128 devices in a mesh: lon: 32 (over y, x_hi, z), band: 4 (over x_lo, core).
Axes of the slice: x: 4 (x_hi: 2, x_lo: 2; x = x_hi * 2 + x_lo), y: 4, z: 4, core: 2. Of those that a mesh axis runs over, the one named last changes fastest.
Arguments:
- denoised_tokens: bfloat16 [4, 32, 7680], P('band', 'lon'), may hold values from -6 to 6
- sequence_row_index: int32 [4, 32], P('band'), may hold values from 0 to 31, each once within a row
- latent_frame_cache: bfloat16 [4, 128, 7680], P(None, 'band', 'lon'), may hold values from -6 to 6
- cache_slot_order: int32 [4], replicated, may hold values from 0 to 3, each once
- temporal_taps_weight: bfloat16 [3, 16, 16], replicated, may hold values from -0.875 to 0.875
- input_weight: bfloat16 [9, 16, 256], replicated, may hold values from -0.5 to 0.5
- latent_conv_weights: bfloat16 [2, 9, 256, 256], replicated, may hold values from -0.125 to 0.125
- upsampled_weight: bfloat16 [9, 256, 256], replicated, may hold values from -0.125 to 0.125
- upper_conv_weights: bfloat16 [2, 9, 256, 256], replicated, may hold values from -0.125 to 0.125
- latent_norm_gains: float32 [2, 256], replicated, may hold values from 0.5 to 1.5
- upper_norm_gains: float32 [2, 256], replicated, may hold values from 0.5 to 1.5
Outputs:
- decoded: bfloat16 [256, 960, 256], P('band', 'lon')
The draws below stay inside these ranges and needn't reach their ends.
Inputs may be any that keep to these rules, and one draw needn't show every extreme that they name: Each row sequence_row_index[b] holds every position 0..31 once. cache_slot_order holds each slot once.
All inputs are finite; a program needn't handle non-finite values.
Results may differ from the reference program's by a relative error of at most 0.02.
Values may be sent and summed in bfloat16 or wider, within the bound.
No kernel may reach another device: no remote copies, remote signals or barrier semaphores. Data moves between devices by JAX's collectives and lax.ppermute only.
A program may use at most 128 MiB of HBM per device.

```python
import jax
import jax.numpy as jnp
from jax import lax

LATENT_CHANNELS = 16
CH = 256
CACHE = 4
BAND_HEIGHT = 32
H = 128
PANORAMA_WIDTH = 480
N_BAND = 4


def levels(key, extent, cuts, smallest, largest):
    def one(axis_at, blocks):
        heights = jax.random.uniform(jax.random.fold_in(jax.random.fold_in(key, 6), axis_at), (blocks,), jnp.float32, smallest / len(cuts), largest / len(cuts))
        return jnp.repeat(jnp.exp(heights), extent[axis_at] // blocks).reshape((-1,) + (1,) * (len(extent) - axis_at - 1))

    loudness = one(*cuts[0])
    for cut in cuts[1:]:
        loudness = loudness * one(*cut)
    return loudness


def centred(key, shape, deviation, most, pieces=(), kind=jnp.bfloat16):
    array = jax.random.normal(key, shape, jnp.float32) * deviation
    if len(pieces) > 0:
        array = levels(key, shape, pieces, -0.22, 0.18) * array
    return jnp.clip(array, min=-most, max=most).astype(kind)


def setup_inputs(seed: int = 0) -> dict:
    key_of = jax.random.split(jax.random.key(seed), 12)
    return {
        "denoised_tokens": centred(key_of[0], (N_BAND, BAND_HEIGHT, PANORAMA_WIDTH * LATENT_CHANNELS), 1.0, 6.0, ((0, 4), (1, 32))),
        "sequence_row_index": jax.vmap(lambda own: jax.random.permutation(own, BAND_HEIGHT))(jax.random.split(key_of[1], N_BAND)).reshape((N_BAND, BAND_HEIGHT)).astype(jnp.int32),
        "latent_frame_cache": centred(key_of[2], (CACHE, H, PANORAMA_WIDTH * LATENT_CHANNELS), 1.0, 6.0, ((1, 4), (2, 32))),
        "cache_slot_order": jax.random.permutation(key_of[3], CACHE).astype(jnp.int32),
        "temporal_taps_weight": centred(key_of[4], (3, LATENT_CHANNELS, LATENT_CHANNELS), (3 * LATENT_CHANNELS) ** -0.5, 0.875),
        "input_weight": centred(key_of[5], (9, LATENT_CHANNELS, CH), (9 * LATENT_CHANNELS) ** -0.5, 0.5),
        "latent_conv_weights": centred(key_of[6], (2, 9, CH, CH), (9 * CH) ** -0.5, 0.125),
        "upsampled_weight": centred(key_of[7], (9, CH, CH), (9 * CH) ** -0.5, 0.125),
        "upper_conv_weights": centred(key_of[8], (2, 9, CH, CH), (9 * CH) ** -0.5, 0.125),
        "latent_norm_gains": jnp.clip(jax.random.uniform(key_of[9], (2, CH), jnp.float32, 0.5, 1.5), 0.5, 1.5),
        "upper_norm_gains": jnp.clip(jax.random.uniform(key_of[10], (2, CH), jnp.float32, 0.5, 1.5), 0.5, 1.5),
    }


def activate(activity, gain_row):
    values = activity.astype(jnp.float32)
    scaled = values * jax.lax.rsqrt(lax.optimization_barrier(jnp.mean(values * values, axis=-1, keepdims=True)) + 1e-06) * gain_row
    return jax.nn.silu(scaled).astype(jnp.bfloat16)

def conv_valid(padded, weight):
    row_count = padded.shape[0] - 2
    col_count = padded.shape[1] - 2
    inputs = padded.shape[2]
    summed = jnp.zeros((row_count * col_count, weight.shape[2]), jnp.float32)
    for offset in range(9):
        shift_row = offset // 3
        shift_col = offset % 3
        window = padded[shift_row:shift_row + row_count, shift_col:shift_col + col_count].reshape(row_count * col_count, inputs)
        summed = summed + jnp.dot(window, weight[offset], preferred_element_type=jnp.float32)
    return summed.reshape(row_count, col_count, weight.shape[2])

def pad_sphere(activity):
    beside_all = jnp.concatenate([activity[:, -1:], activity, activity[:, :1]], axis=1)
    border = jnp.zeros((1,) + beside_all.shape[1:], activity.dtype)
    return jnp.concatenate([border, beside_all, border], axis=0)

def conv_full(activity, weight):
    return conv_valid(pad_sphere(activity), weight)

def res_block(activity, gain_rows, weights):
    inner_sum = conv_full(activate(activity, gain_rows[0]), weights[0])
    branch = conv_full(activate(inner_sum, gain_rows[1]), weights[1])
    return (activity.astype(jnp.float32) + branch).astype(jnp.bfloat16)

def reference(denoised_tokens, sequence_row_index, latent_frame_cache, cache_slot_order, temporal_taps_weight, input_weight, latent_conv_weights, upsampled_weight, upper_conv_weights, latent_norm_gains, upper_norm_gains):
    sorted_rows = jax.vmap(lambda token_rows, row_places: token_rows[row_places])(denoised_tokens, sequence_row_index)
    latent = sorted_rows.reshape(H * PANORAMA_WIDTH, LATENT_CHANNELS)
    newest = latent_frame_cache[cache_slot_order[0]].reshape(H * PANORAMA_WIDTH, LATENT_CHANNELS)
    oldest = latent_frame_cache[cache_slot_order[1]].reshape(H * PANORAMA_WIDTH, LATENT_CHANNELS)
    mixture = jnp.dot(latent, temporal_taps_weight[0], preferred_element_type=jnp.float32)
    mixture = mixture + jnp.dot(newest, temporal_taps_weight[1], preferred_element_type=jnp.float32)
    mixture = mixture + jnp.dot(oldest, temporal_taps_weight[2], preferred_element_type=jnp.float32)
    temporal = mixture.astype(jnp.bfloat16).reshape(H, PANORAMA_WIDTH, LATENT_CHANNELS)
    opening = conv_full(temporal, input_weight).astype(jnp.bfloat16)
    low_res = res_block(opening, latent_norm_gains, latent_conv_weights)
    upsampled = jnp.repeat(jnp.repeat(low_res, 2, axis=0), 2, axis=1)
    high_res = conv_full(upsampled, upsampled_weight).astype(jnp.bfloat16)
    return res_block(high_res, upper_norm_gains, upper_conv_weights)
```

```python
import functools

import jax
import jax.numpy as jnp
from jax import lax
from jax.experimental import pallas as pl
from jax.experimental.pallas import tpu as pltpu
from jax.sharding import PartitionSpec as P

F32 = jnp.float32
BF16 = jnp.bfloat16

N_LON = 32
N_BAND = 4
N_DEV = N_LON * N_BAND
ROWS = 32
COLS = 15
LAT = 16
CH = 256
HALO = 5
TOKEN = 480 * LAT
LANES = COLS * LAT
EDGE = HALO * LAT
WINDOW = LANES + 2 * EDGE
CHUNK = 24


def window_start(lon):
    return (LANES * lon - EDGE) // 128


def window_offset(lon):
    return (LANES * lon - EDGE) % 128


def iota(shape, dim):
    return lax.broadcasted_iota(jnp.int32, shape, dim)


def block_diagonal(tap):
    rows = jnp.where(iota((128, LAT), 0) % LAT == iota((128, LAT), 1), 1.0, 0.0).astype(BF16)
    cols = jnp.where(iota((LAT, 128), 1) % LAT == iota((LAT, 128), 0), 1.0, 0.0).astype(BF16)
    tall = jnp.dot(rows, tap, preferred_element_type=F32).astype(BF16)
    full = jnp.dot(tall, cols, preferred_element_type=F32)
    same = iota((128, 128), 0) // LAT == iota((128, 128), 1) // LAT
    return jnp.where(same, full, 0.0).astype(BF16)


def pack_kernel(index_ref, slot_ref, token_ref, cache_ref, taps_ref, send_ref, own_ref, x_ref):
    lon = lax.axis_index("lon")
    band = lax.axis_index("band")
    row = jnp.int32(0)
    for r in range(ROWS):
        row = jnp.where(index_ref[0, r] == lon, r, row)
    tag = row.astype(F32)
    for k in range(TOKEN // 128):
        piece = token_ref[0, :, 128 * k : 128 * k + 128].astype(F32)
        x_ref[k : k + 1, :] = piece
        if k < 4:
            x_ref[60 + k : 61 + k, :] = piece
    place = iota((8, 128), 0) * 128 + iota((8, 128), 1)
    for target in range(N_LON):
        start = window_start(target) % 60
        spot = (window_offset(target) + WINDOW) % 512
        tile = x_ref[start : start + 8, :]
        tile = jnp.where(place == spot, tag, tile).astype(BF16)
        for b in range(N_BAND):
            send_ref[target * N_BAND + b, 0:8, :] = tile

    diagonals = [block_diagonal(taps_ref[t]) for t in (1, 2)]
    mixed = jnp.zeros((2 * ROWS, 128), F32)
    for t in range(2):
        frame = cache_ref[slot_ref[t]]
        frame = jnp.concatenate([frame, jnp.zeros((ROWS, 256 - LANES), BF16)], axis=1)
        stacked = jnp.concatenate([frame[:, :128], frame[:, 128:]], axis=0)
        mixed = mixed + jnp.dot(stacked, diagonals[t], preferred_element_type=F32)
    own = jnp.concatenate([mixed[:ROWS], mixed[ROWS:]], axis=1)
    own_ref[...] = own

    def send(d_lon, d_band, part):
        rest = CHUNK - 4 - part.shape[0]
        full = [jnp.zeros((4, 128), F32), part]
        if rest:
            full.append(jnp.zeros((rest, 128), F32))
        full = jnp.concatenate(full, axis=0)
        to = lax.rem(lon + d_lon + N_LON, N_LON) * N_BAND + lax.rem(band + d_band + N_BAND, N_BAND)
        first = send_ref[to, 0:8, :].astype(F32)
        send_ref[to, 0:8, :] = jnp.where(iota((8, 128), 0) < 4, first, full[:8]).astype(BF16)
        send_ref[to, 8:CHUNK, :] = full[8:].astype(BF16)

    def tall(v):
        top = jnp.concatenate([v[:16, :EDGE], v[16:, : 128 - EDGE]], axis=1)
        low = jnp.concatenate(
            [v[16 + 4 * m : 20 + 4 * m, 128 - EDGE : EDGE] for m in range(4)], axis=1
        )
        return jnp.concatenate([top, low], axis=0)

    def corner(v):
        return jnp.concatenate([v, jnp.zeros((HALO, 128 - EDGE), F32)], axis=1)

    left, right = own[:, :EDGE], own[:, LANES - EDGE : LANES]
    send(-1, 0, tall(left))
    send(1, 0, tall(right))
    for d_band, rows in ((-1, slice(0, HALO)), (1, slice(ROWS - HALO, ROWS))):
        wide = own[rows]
        send(0, d_band, jnp.concatenate([wide[:, :128], wide[:, 128:]], axis=0))
        send(-1, d_band, corner(left[rows]))
        send(1, d_band, corner(right[rows]))


def activate(values, gain):
    mean = jnp.sum(values * values, axis=-1, keepdims=True) * (1.0 / CH)
    half = values * lax.rsqrt(mean + 1e-06) * (0.5 * gain)
    return half * jnp.tanh(half) + half


def roll_rows(values, by):
    return pltpu.roll(values, by % values.shape[0], axis=0)


LOW = 32
HIGH = 16


def block_kernel(
    got_ref,
    own_ref,
    taps_ref,
    low_gain_ref,
    high_gain_ref,
    w_in_hbm,
    w_low_hbm,
    w_up_hbm,
    w_high_hbm,
    out_hbm,
    w_in,
    w_low,
    w_up,
    w_high,
    w_phase,
    tok_ref,
    u_ref,
    open_ref,
    a1_ref,
    a2_ref,
    low_ref,
    s1_ref,
    raw_ref,
    s2_ref,
    mix_ref,
    out_ref,
    in_sem,
    out_sem,
):
    lon = lax.axis_index("lon")
    band = lax.axis_index("band")
    copies = [pltpu.make_async_copy(w_in_hbm.at[p], w_in.at[p, 0:48], in_sem.at[p]) for p in range(3)]
    copies.append(pltpu.make_async_copy(w_low_hbm.at[0], w_low.at[0], in_sem.at[3]))
    copies.append(pltpu.make_async_copy(w_low_hbm.at[1], w_low.at[1], in_sem.at[4]))
    copies.append(pltpu.make_async_copy(w_up_hbm, w_up, in_sem.at[5]))
    copies.append(pltpu.make_async_copy(w_high_hbm.at[0], w_high.at[0], in_sem.at[6]))
    copies.append(pltpu.make_async_copy(w_high_hbm.at[1], w_high.at[1], in_sem.at[7]))
    w_in[:, 48:128, :] = jnp.zeros((3, 80, CH), BF16)
    for copy in copies:
        copy.start()

    tok_ref[...] = got_ref[:, 0:8, :].astype(F32).reshape(N_DEV * 8, 128)
    x = jnp.concatenate([tok_ref[pl.ds(k, N_DEV, stride=8), :] for k in range(4)], axis=1)
    offset = lax.rem(LANES * lon + (128 - EDGE), 128)
    x = pltpu.roll(x, lax.rem(512 - offset, 512), axis=1)
    tag = x[:, WINDOW : WINDOW + 1].astype(jnp.int32)
    m = iota((N_DEV, 128), 1)
    want_band = jnp.where(m < HALO, band - 1, jnp.where(m < HALO + ROWS, band, band + 1))
    want_row = jnp.where(
        m < HALO, m + ROWS - HALO, jnp.where(m < HALO + ROWS, m - HALO, m - HALO - ROWS)
    )
    want_row = jnp.where(m < 2 * HALO + ROWS, want_row, -1)
    hit = (tag == want_row) & (iota((N_DEV, 128), 0) % N_BAND == want_band)
    select = jnp.where(hit, 1.0, 0.0).T[:48].astype(BF16)
    latent = jnp.dot(select, x.astype(BF16), preferred_element_type=F32).astype(BF16)

    def chunk(d_lon, d_band):
        source = lax.rem(lon + d_lon + N_LON, N_LON) * N_BAND + lax.rem(band + d_band + N_BAND, N_BAND)
        return got_ref[source].astype(F32)[4:]

    def side(d_lon):
        c = chunk(d_lon, 0)
        low = jnp.concatenate([c[16:20, 32 * k : 32 * k + 32] for k in range(4)], axis=0)
        low = jnp.concatenate([c[:16, EDGE:], low], axis=1)
        return jnp.concatenate([c[:16, :EDGE], low], axis=0)

    def rim(d_band):
        c = chunk(0, d_band)
        parts = [
            chunk(-1, d_band)[:HALO, :EDGE],
            c[:HALO],
            c[HALO : 2 * HALO, : LANES - 128],
            chunk(1, d_band)[:HALO, :EDGE],
            jnp.zeros((HALO, 512 - WINDOW), F32),
        ]
        whole = jnp.concatenate(parts, axis=1)
        inside = (band + d_band >= 0) & (band + d_band < N_BAND)
        return jnp.where(inside, whole, 0.0)

    middle = jnp.concatenate(
        [side(-1), own_ref[:, :LANES], side(1), jnp.zeros((ROWS, 512 - WINDOW), F32)], axis=1
    )
    cached = jnp.concatenate([rim(-1), middle, rim(1), jnp.zeros((6, 512), F32)], axis=0)
    diagonal = block_diagonal(taps_ref[0])
    stacked = jnp.concatenate([latent[:, 128 * k : 128 * k + 128] for k in range(4)], axis=0)
    fresh = jnp.dot(stacked, diagonal, preferred_element_type=F32)
    fresh = jnp.concatenate([fresh[48 * k : 48 * k + 48] for k in range(4)], axis=1)
    temporal = (fresh + cached).astype(BF16).astype(F32)
    temporal = jnp.where(iota((48, 512), 1) < WINDOW, temporal, 0.0)

    wide = jnp.concatenate([temporal, jnp.zeros((48, 128), F32)], axis=1)
    for j in range(24):
        piece = wide[:, 128 * (j // 8) : 128 * (j // 8) + 256]
        turn = LAT * (j % 8)
        if turn:
            piece = pltpu.roll(piece, 256 - turn, axis=1)
        u_ref[j] = piece[:, :128]
    lhs = jnp.concatenate(
        [u_ref[:, p : p + 40, :].reshape(960, 128).astype(BF16) for p in range(3)], axis=1
    )
    for copy in copies[:3]:
        copy.wait()
    opening = jnp.dot(lhs, w_in[...].reshape(384, CH), preferred_element_type=F32)
    opening = opening.astype(BF16).astype(F32)
    for j in range(23):
        for half in range(2):
            open_ref[half, pl.ds(j, 40, stride=LOW), :] = opening[
                40 * j : 40 * j + 40, 128 * half : 128 * half + 128
            ]

    def opened(rows):
        return jnp.concatenate([open_ref[0, rows, :], open_ref[1, rows, :]], axis=1)

    def zero_rows(ref, pitch, top, bottom):
        total = ref.shape[0] // pitch

        @pl.when(band == 0)
        def _():
            ref[0 : top * pitch, :] = jnp.zeros((top * pitch, ref.shape[1]), ref.dtype)

        @pl.when(band == N_BAND - 1)
        def _():
            ref[(total - bottom) * pitch :, :] = jnp.zeros((bottom * pitch, ref.shape[1]), ref.dtype)

    def conv(ref, pitch, row, count, lane, weight):
        total = None
        for p in range(3):
            part = jnp.dot(
                ref[(row + p) * pitch : (row + p + count) * pitch, lane : lane + 3 * CH],
                weight[p],
                preferred_element_type=F32,
            )
            total = part if total is None else total + part
        return total

    def spread(act, ref, at):
        rows = slice(at, at + act.shape[0])
        ref[rows, 0:CH] = roll_rows(act, 1).astype(BF16)
        ref[rows, CH : 2 * CH] = act.astype(BF16)
        ref[rows, 2 * CH :] = roll_rows(act, -1).astype(BF16)

    gain = low_gain_ref[0:1, :]
    for r in range(0, 40, 10):
        rows = slice(r * LOW, (r + 10) * LOW)
        spread(activate(opened(rows), gain), a1_ref, r * LOW)
    zero_rows(a1_ref, LOW, 4, 4)
    copies[3].wait()
    gain = low_gain_ref[1:2, :]
    for r in range(0, 38, 19):
        inner = conv(a1_ref, LOW, r, 19, 0, w_low.at[0])
        spread(activate(inner, gain), a2_ref, r * LOW)
    zero_rows(a2_ref, LOW, 3, 3)
    copies[4].wait()
    for r in range(0, 36, 18):
        branch = conv(a2_ref, LOW, r, 18, 0, w_low.at[1])
        low = opened(slice((r + 2) * LOW, (r + 20) * LOW)) + branch
        for k in range(4):
            part = roll_rows(low, -(2 + k)).reshape(18, LOW, CH)[:, :HIGH]
            low_ref[r * HIGH : (r + 18) * HIGH, CH * k : CH * k + CH] = part.reshape(
                18 * HIGH, CH
            ).astype(BF16)
    zero_rows(low_ref, HIGH, 2, 2)

    copies[5].wait()
    for a in range(2):
        for r in range(2):
            taps = ((0,), (1, 2)) if a == 0 else ((0, 1), (2,))
            for odd in range(2):
                sides = ((0, 1), (2,)) if odd else ((0,), (1, 2))
                for c in range(2):
                    total = None
                    for p in taps[r]:
                        for q in sides[c]:
                            one = w_up[3 * p + q].astype(F32)
                            total = one if total is None else total + one
                    w_phase[a, r, CH * c : CH * c + CH, (1 - odd) * CH : (2 - odd) * CH] = (
                        total.astype(BF16)
                    )
    gain = high_gain_ref[0:1, :]
    for a in range(2):
        for n in range(0, 34, 17):

            def phase(lane, out_lane, width):
                total = None
                for r in range(2):
                    at = (n + a + r) * HIGH
                    part = jnp.dot(
                        low_ref[at : at + 17 * HIGH, lane : lane + 2 * CH],
                        w_phase[a, r, :, out_lane : out_lane + width],
                        preferred_element_type=F32,
                    )
                    total = part if total is None else total + part
                return total.astype(BF16).astype(F32)

            def put(value, slot, raw_slot):
                act = activate(value, gain).astype(BF16)
                raw = value.astype(BF16)
                for i in range(17):
                    at = (2 * (n + i) + a) * HIGH
                    rows = slice(i * HIGH, (i + 1) * HIGH)
                    s1_ref[at : at + HIGH, CH * slot : CH * slot + CH] = act[rows]
                    if raw_slot is not None:
                        raw_ref[at : at + HIGH, CH * raw_slot : CH * raw_slot + CH] = raw[rows]

            both = phase(CH, 0, 2 * CH)
            put(both[:, :CH], 1, None)
            put(both[:, CH:], 2, 0)
            put(phase(2 * CH, 0, CH), 3, 1)
            put(phase(0, CH, CH), 0, None)
    zero_rows(s1_ref, HIGH, 2, 2)

    copies[6].wait()
    gain = high_gain_ref[1:2, :]
    for r in range(0, 66, 22):
        rows = slice(r * HIGH, (r + 22) * HIGH)
        odd = activate(conv(s1_ref, HIGH, r, 22, 0, w_high.at[0]), gain)
        s2_ref[rows, 0:CH] = odd.astype(BF16)
        s2_ref[rows, 2 * CH : 3 * CH] = roll_rows(odd, -1).astype(BF16)
        even = activate(conv(s1_ref, HIGH, r, 22, CH, w_high.at[0]), gain)
        s2_ref[rows, CH : 2 * CH] = even.astype(BF16)
        s2_ref[rows, 3 * CH :] = roll_rows(even, -1).astype(BF16)
    zero_rows(s2_ref, HIGH, 1, 1)
    copies[7].wait()
    outs = []
    for n, r in enumerate(range(0, 64, 16)):
        rows = slice((r + 2) * HIGH, (r + 18) * HIGH)
        even = conv(s2_ref, HIGH, r, 16, 0, w_high.at[1]) + raw_ref[rows, :CH].astype(F32)
        odd = conv(s2_ref, HIGH, r, 16, CH, w_high.at[1]) + raw_ref[rows, CH:].astype(F32)
        for half in range(2):
            lanes = slice(128 * half, 128 * half + 128)
            mix_ref[n % 2, half, pl.ds(0, 16 * HIGH, stride=2), :] = even[:, lanes]
            mix_ref[n % 2, half, pl.ds(1, 16 * HIGH, stride=2), :] = odd[:, lanes]
            out_ref[r : r + 16, :, lanes] = (
                mix_ref[n % 2, half].astype(BF16).reshape(16, 32, 128)[:, :30]
            )
        copy = pltpu.make_async_copy(
            out_ref.at[r : r + 16], out_hbm.at[r : r + 16], out_sem.at[n]
        )
        copy.start()
        outs.append(copy)
    for copy in outs:
        copy.wait()


def shards(
    denoised_tokens,
    sequence_row_index,
    latent_frame_cache,
    cache_slot_order,
    temporal_taps_weight,
    input_weight,
    latent_conv_weights,
    upsampled_weight,
    upper_conv_weights,
    latent_norm_gains,
    upper_norm_gains,
):
    struct = jax.ShapeDtypeStruct
    vmem = pl.BlockSpec(memory_space=pltpu.VMEM)
    smem = pl.BlockSpec(memory_space=pltpu.SMEM)
    anywhere = pl.BlockSpec(memory_space=pl.ANY)
    payload, own = pl.pallas_call(
        pack_kernel,
        in_specs=[smem, smem, vmem, vmem, vmem],
        out_specs=[vmem, vmem],
        out_shape=[struct((N_DEV, CHUNK, 128), BF16), struct((ROWS, 256), F32)],
        scratch_shapes=[pltpu.VMEM((72, 128), F32)],
        name="pack",
    )(
        sequence_row_index,
        cache_slot_order,
        denoised_tokens,
        latent_frame_cache,
        temporal_taps_weight,
    )
    arrived = lax.all_to_all(payload, ("lon", "band"), 0, 0, tiled=True)
    return pl.pallas_call(
        block_kernel,
        in_specs=[vmem] * 5 + [anywhere] * 4,
        out_specs=anywhere,
        out_shape=struct((2 * ROWS, 2 * COLS, CH), BF16),
        scratch_shapes=[
            pltpu.VMEM((3, 128, CH), BF16),
            pltpu.VMEM((2, 3, 3 * CH, CH), BF16),
            pltpu.VMEM((9, CH, CH), BF16),
            pltpu.VMEM((2, 3, 3 * CH, CH), BF16),
            pltpu.VMEM((2, 2, 2 * CH, 2 * CH), BF16),
            pltpu.VMEM((N_DEV * 8, 128), F32),
            pltpu.VMEM((24, 48, 128), F32),
            pltpu.VMEM((2, 40 * LOW, 128), F32),
            pltpu.VMEM((40 * LOW, 3 * CH), BF16),
            pltpu.VMEM((38 * LOW, 3 * CH), BF16),
            pltpu.VMEM((36 * HIGH, 4 * CH), BF16),
            pltpu.VMEM((68 * HIGH, 4 * CH), BF16),
            pltpu.VMEM((68 * HIGH, 2 * CH), BF16),
            pltpu.VMEM((66 * HIGH, 4 * CH), BF16),
            pltpu.VMEM((2, 2, 2 * 16 * HIGH, 128), F32),
            pltpu.VMEM((2 * ROWS, 2 * COLS, CH), BF16),
            pltpu.SemaphoreType.DMA((8,)),
            pltpu.SemaphoreType.DMA((4,)),
        ],
        compiler_params=pltpu.CompilerParams(vmem_limit_bytes=50 * 1024 * 1024),
        name="block",
    )(
        arrived,
        own,
        temporal_taps_weight,
        latent_norm_gains,
        upper_norm_gains,
        input_weight.reshape(3, 48, CH),
        latent_conv_weights.reshape(2, 3, 3 * CH, CH),
        upsampled_weight,
        upper_conv_weights.reshape(2, 3, 3 * CH, CH),
    )


def solution(mesh):
    in_specs = (
        P("band", "lon", None),
        P("band", None),
        P(None, "band", "lon"),
        P(),
        P(),
        P(),
        P(),
        P(),
        P(),
        P(),
        P(),
    )
    out_specs = P("band", "lon", None)
    return jax.shard_map(shards, mesh=mesh, in_specs=in_specs, out_specs=out_specs, check_vma=False)
```

```python
import functools

import jax
import jax.numpy as jnp
from jax import lax
from jax.experimental import pallas as pl
from jax.experimental.pallas import tpu as pltpu
from jax.sharding import PartitionSpec as P

F32 = jnp.float32
BF16 = jnp.bfloat16

N_LON = 32
N_BAND = 4
N_DEV = N_LON * N_BAND
ROWS = 32
COLS = 15
LAT = 16
CH = 256
HALO = 5
TOKEN = 480 * LAT
LANES = COLS * LAT
EDGE = HALO * LAT
WINDOW = LANES + 2 * EDGE
CHUNK = 24


def window_start(lon):
    return (LANES * lon - EDGE) // 128


def window_offset(lon):
    return (LANES * lon - EDGE) % 128


def iota(shape, dim):
    return lax.broadcasted_iota(jnp.int32, shape, dim)


def block_diagonal(tap):
    rows = jnp.where(iota((128, LAT), 0) % LAT == iota((128, LAT), 1), 1.0, 0.0).astype(BF16)
    cols = jnp.where(iota((LAT, 128), 1) % LAT == iota((LAT, 128), 0), 1.0, 0.0).astype(BF16)
    tall = jnp.dot(rows, tap, preferred_element_type=F32).astype(BF16)
    full = jnp.dot(tall, cols, preferred_element_type=F32)
    same = iota((128, 128), 0) // LAT == iota((128, 128), 1) // LAT
    return jnp.where(same, full, 0.0).astype(BF16)


def pack_kernel(index_ref, slot_ref, token_ref, cache_ref, taps_ref, send_ref, own_ref, x_ref):
    lon = lax.axis_index("lon")
    band = lax.axis_index("band")
    row = jnp.int32(0)
    for r in range(ROWS):
        row = jnp.where(index_ref[0, r] == lon, r, row)
    tag = row.astype(F32)
    for k in range(TOKEN // 128):
        piece = token_ref[0, :, 128 * k : 128 * k + 128].astype(F32)
        x_ref[k : k + 1, :] = piece
        if k < 4:
            x_ref[60 + k : 61 + k, :] = piece
    place = iota((8, 128), 0) * 128 + iota((8, 128), 1)
    for target in range(N_LON):
        start = window_start(target) % 60
        spot = (window_offset(target) + WINDOW) % 512
        tile = x_ref[start : start + 8, :]
        tile = jnp.where(place == spot, tag, tile).astype(BF16)
        for b in range(N_BAND):
            send_ref[target * N_BAND + b, 0:8, :] = tile

    diagonals = [block_diagonal(taps_ref[t]) for t in (1, 2)]
    mixed = jnp.zeros((2 * ROWS, 128), F32)
    for t in range(2):
        frame = cache_ref[slot_ref[t]]
        frame = jnp.concatenate([frame, jnp.zeros((ROWS, 256 - LANES), BF16)], axis=1)
        stacked = jnp.concatenate([frame[:, :128], frame[:, 128:]], axis=0)
        mixed = mixed + jnp.dot(stacked, diagonals[t], preferred_element_type=F32)
    own = jnp.concatenate([mixed[:ROWS], mixed[ROWS:]], axis=1)
    own_ref[...] = own

    def send(d_lon, d_band, part):
        rest = CHUNK - 4 - part.shape[0]
        full = [jnp.zeros((4, 128), F32), part]
        if rest:
            full.append(jnp.zeros((rest, 128), F32))
        full = jnp.concatenate(full, axis=0)
        to = lax.rem(lon + d_lon + N_LON, N_LON) * N_BAND + lax.rem(band + d_band + N_BAND, N_BAND)
        first = send_ref[to, 0:8, :].astype(F32)
        send_ref[to, 0:8, :] = jnp.where(iota((8, 128), 0) < 4, first, full[:8]).astype(BF16)
        send_ref[to, 8:CHUNK, :] = full[8:].astype(BF16)

    def tall(v):
        top = jnp.concatenate([v[:16, :EDGE], v[16:, : 128 - EDGE]], axis=1)
        low = jnp.concatenate(
            [v[16 + 4 * m : 20 + 4 * m, 128 - EDGE : EDGE] for m in range(4)], axis=1
        )
        return jnp.concatenate([top, low], axis=0)

    def corner(v):
        return jnp.concatenate([v, jnp.zeros((HALO, 128 - EDGE), F32)], axis=1)

    left, right = own[:, :EDGE], own[:, LANES - EDGE : LANES]
    send(-1, 0, tall(left))
    send(1, 0, tall(right))
    for d_band, rows in ((-1, slice(0, HALO)), (1, slice(ROWS - HALO, ROWS))):
        wide = own[rows]
        send(0, d_band, jnp.concatenate([wide[:, :128], wide[:, 128:]], axis=0))
        send(-1, d_band, corner(left[rows]))
        send(1, d_band, corner(right[rows]))


def activate(values, gain):
    mean = jnp.sum(values * values, axis=-1, keepdims=True) * (1.0 / CH)
    half = values * lax.rsqrt(mean + 1e-06) * (0.5 * gain)
    return half * jnp.tanh(half) + half


def roll_rows(values, by):
    return pltpu.roll(values, by % values.shape[0], axis=0)


def cuts(rows, pieces):
    ends = [rows * k // pieces for k in range(pieces + 1)]
    return [(low, high - low) for low, high in zip(ends[:-1], ends[1:])]


LOW = 24
HIGH = 16


def block_kernel(
    got_hbm,
    own_hbm,
    taps_hbm,
    low_gain_hbm,
    high_gain_hbm,
    w_in_hbm,
    w_low_hbm,
    w_up_hbm,
    w_high_hbm,
    out_hbm,
    got_ref,
    near_ref,
    own_ref,
    taps_ref,
    low_gain_ref,
    high_gain_ref,
    w_in,
    w_low,
    w_up,
    w_high,
    w_phase,
    tok_ref,
    u_ref,
    open_ref,
    a1_ref,
    a2_ref,
    low_ref,
    lowf_ref,
    s1_ref,
    raw_ref,
    s2_ref,
    mix_ref,
    done_ref,
    out_ref,
    in_sem,
    out_sem,
):
    lon = lax.axis_index("lon")
    band = lax.axis_index("band")
    copies = [pltpu.make_async_copy(w_in_hbm.at[p], w_in.at[p, 0:48], in_sem.at[p]) for p in range(3)]
    copies.append(pltpu.make_async_copy(w_low_hbm.at[0], w_low.at[0], in_sem.at[3]))
    copies.append(pltpu.make_async_copy(w_low_hbm.at[1], w_low.at[1], in_sem.at[4]))
    copies.append(pltpu.make_async_copy(w_up_hbm, w_up, in_sem.at[5]))
    copies.append(pltpu.make_async_copy(w_high_hbm.at[0], w_high.at[0], in_sem.at[6]))
    copies.append(pltpu.make_async_copy(w_high_hbm.at[1], w_high.at[1], in_sem.at[7]))
    small = [
        pltpu.make_async_copy(source, target, in_sem.at[8 + n])
        for n, (source, target) in enumerate(
            (
                (own_hbm, own_ref),
                (taps_hbm, taps_ref),
                (low_gain_hbm, low_gain_ref),
                (high_gain_hbm, high_gain_ref),
            )
        )
    ]
    tokens = pltpu.make_async_copy(got_hbm.at[:, 0:8], got_ref, in_sem.at[12])
    around = [(l, b) for b in (-1, 0, 1) for l in (-1, 0, 1) if l or b]
    for n, (l, b) in enumerate(around):
        source = lax.rem(lon + l + N_LON, N_LON) * N_BAND + lax.rem(band + b + N_BAND, N_BAND)
        small.append(
            pltpu.make_async_copy(got_hbm.at[source], near_ref.at[n], in_sem.at[13 + n])
        )
    for copy in [tokens] + small + copies:
        copy.start()
    w_in[:, 48:128, :] = jnp.zeros((3, 80, CH), BF16)

    tokens.wait()
    tok_ref[...] = got_ref[...].astype(F32).reshape(N_DEV * 8, 128)
    x = jnp.concatenate([tok_ref[pl.ds(k, N_DEV, stride=8), :] for k in range(4)], axis=1)
    offset = lax.rem(LANES * lon + (128 - EDGE), 128)
    x = pltpu.roll(x, lax.rem(512 - offset, 512), axis=1)
    tag = x[:, WINDOW : WINDOW + 1].astype(jnp.int32)
    m = iota((N_DEV, 128), 1)
    want_band = jnp.where(m < HALO, band - 1, jnp.where(m < HALO + ROWS, band, band + 1))
    want_row = jnp.where(
        m < HALO, m + ROWS - HALO, jnp.where(m < HALO + ROWS, m - HALO, m - HALO - ROWS)
    )
    want_row = jnp.where(m < 2 * HALO + ROWS, want_row, -1)
    hit = (tag == want_row) & (iota((N_DEV, 128), 0) % N_BAND == want_band)
    select = jnp.where(hit, 1.0, 0.0).T[:48].astype(BF16)
    latent = jnp.dot(select, x.astype(BF16), preferred_element_type=F32).astype(BF16)

    for copy in small:
        copy.wait()

    def chunk(d_lon, d_band):
        return near_ref[around.index((d_lon, d_band))].astype(F32)[4:]

    def side(d_lon):
        c = chunk(d_lon, 0)
        low = jnp.concatenate([c[16:20, 32 * k : 32 * k + 32] for k in range(4)], axis=0)
        low = jnp.concatenate([c[:16, EDGE:], low], axis=1)
        return jnp.concatenate([c[:16, :EDGE], low], axis=0)

    def rim(d_band):
        c = chunk(0, d_band)
        parts = [
            chunk(-1, d_band)[:HALO, :EDGE],
            c[:HALO],
            c[HALO : 2 * HALO, : LANES - 128],
            chunk(1, d_band)[:HALO, :EDGE],
            jnp.zeros((HALO, 512 - WINDOW), F32),
        ]
        whole = jnp.concatenate(parts, axis=1)
        inside = (band + d_band >= 0) & (band + d_band < N_BAND)
        return jnp.where(inside, whole, 0.0)

    middle = jnp.concatenate(
        [side(-1), own_ref[:, :LANES], side(1), jnp.zeros((ROWS, 512 - WINDOW), F32)], axis=1
    )
    cached = jnp.concatenate([rim(-1), middle, rim(1), jnp.zeros((6, 512), F32)], axis=0)
    diagonal = block_diagonal(taps_ref[0])
    stacked = jnp.concatenate([latent[:, 128 * k : 128 * k + 128] for k in range(4)], axis=0)
    fresh = jnp.dot(stacked, diagonal, preferred_element_type=F32)
    fresh = jnp.concatenate([fresh[48 * k : 48 * k + 48] for k in range(4)], axis=1)
    temporal = (fresh + cached).astype(BF16).astype(F32)
    temporal = jnp.where(iota((48, 512), 1) < WINDOW, temporal, 0.0)

    wide = jnp.concatenate([temporal, jnp.zeros((48, 128), F32)], axis=1)
    for j in range(LOW):
        piece = wide[:, 128 * (j // 8) : 128 * (j // 8) + 256]
        turn = LAT * (j % 8)
        if turn:
            piece = pltpu.roll(piece, 256 - turn, axis=1)
        u_ref[pl.ds(j, 48, stride=LOW), :] = piece[:, :128]

    def outside(value, pitch, row, top, bottom, rows):
        count = value.shape[0] // pitch
        above = min(max(top - row, 0), count)
        below = min(max(row + count - (rows - bottom), 0), count)
        parts = []
        if above:
            parts.append(jnp.where(band == 0, 0.0, value[: above * pitch]))
        parts.append(value[above * pitch : (count - below) * pitch])
        if below:
            parts.append(jnp.where(band == N_BAND - 1, 0.0, value[(count - below) * pitch :]))
        return parts[0] if len(parts) == 1 else jnp.concatenate(parts, axis=0)

    def conv(ref, pitch, row, count, lane, weight):
        total = None
        for p in range(3):
            part = jnp.dot(
                ref[(row + p) * pitch : (row + p + count) * pitch, lane : lane + 3 * CH],
                weight[p],
                preferred_element_type=F32,
            )
            total = part if total is None else total + part
        return total

    def spread(act, ref, row):
        rows = slice(row * LOW, row * LOW + act.shape[0])
        ref[rows, 0:CH] = roll_rows(act, 1).astype(BF16)
        ref[rows, CH : 2 * CH] = act.astype(BF16)
        ref[rows, 2 * CH :] = roll_rows(act, -1).astype(BF16)

    tasks = []

    def task(product, finish, wait=None):
        tasks.append((product, finish, wait))

    for row, count in cuts(40, 4):

        def product(row=row, count=count):
            lhs = [u_ref[(row + p) * LOW : (row + p + count) * LOW, :] for p in range(3)]
            lhs = jnp.concatenate(lhs, axis=1).astype(BF16)
            return jnp.dot(lhs, w_in[...].reshape(384, CH), preferred_element_type=F32)

        def finish(value, row=row, count=count):
            value = value.astype(BF16).astype(F32)
            open_ref[row * LOW : (row + count) * LOW, :] = value
            act = activate(value, low_gain_ref[0:1, :])
            spread(outside(act, LOW, row, 4, 4, 40), a1_ref, row)

        task(product, finish, copies[:3] if row == 0 else None)

    for row, count in cuts(38, 4):

        def product(row=row, count=count):
            return conv(a1_ref, LOW, row, count, 0, w_low.at[0])

        def finish(value, row=row):
            act = activate(value, low_gain_ref[1:2, :])
            spread(outside(act, LOW, row, 3, 3, 38), a2_ref, row)

        task(product, finish, copies[3:4] if row == 0 else None)

    for row, count in cuts(36, 4):

        def product(row=row, count=count):
            return conv(a2_ref, LOW, row, count, 0, w_low.at[1])

        def finish(value, row=row, count=count):
            low = open_ref[(row + 2) * LOW : (row + 2 + count) * LOW, :] + value
            low = outside(low.astype(BF16).astype(F32), LOW, row, 2, 2, 36)
            for half in range(2):
                lowf_ref[half, row * LOW : (row + count) * LOW, :] = low[
                    :, 128 * half : 128 * half + 128
                ]
            for k in range(2):
                part = roll_rows(low, -(3 + k)).reshape(count, LOW, CH)[:, :HIGH]
                low_ref[row * HIGH : (row + count) * HIGH, CH * k : CH * k + CH] = part.reshape(
                    count * HIGH, CH
                ).astype(BF16)

        task(product, finish, copies[4:5] if row == 0 else None)

    def phase_weights(a, odd):
        for r in range(2):
            taps = ((0,), (1, 2)) if a == 0 else ((0, 1), (2,))
            sides = ((0, 1), (2,)) if odd else ((0,), (1, 2))
            for c in range(2):
                total = None
                for p in taps[r]:
                    for q in sides[c]:
                        one = w_up[3 * p + q].astype(F32)
                        total = one if total is None else total + one
                at = (2 * r + c) * CH
                w_phase[a, odd, at : at + CH, :] = total.astype(BF16)

    for n in (0, 17):
        for a in range(2):
            for odd in range(2):

                def product(n=n, a=a, odd=odd):
                    parts = []
                    for r in range(2):
                        at = n + a + r
                        col = 19 if odd else 2
                        pair = [
                            lowf_ref[half, pl.ds(at * LOW + col + c, 24, stride=LOW), :]
                            for c in range(2)
                            for half in range(2)
                        ]
                        pair = jnp.concatenate(pair, axis=1).astype(BF16)
                        main = low_ref[at * HIGH : (at + 17) * HIGH, :]
                        pad = jnp.zeros((8, 2 * CH), BF16)
                        parts.append(jnp.concatenate([main, pair, pad], axis=0))
                    return jnp.dot(
                        jnp.concatenate(parts, axis=1),
                        w_phase[a, odd],
                        preferred_element_type=F32,
                    )

                def finish(value, n=n, a=a, odd=odd):
                    value = value[: 17 * HIGH + 24].astype(BF16)
                    act = activate(value.astype(F32), high_gain_ref[0:1, :])
                    border = act[17 * HIGH :]
                    act = act[: 17 * HIGH]
                    turned = roll_rows(act, -1 if odd else 1)
                    for half in range(2):
                        lanes = slice(128 * half, 128 * half + 128)
                        mix_ref[odd, half, 0 : 17 * HIGH, :] = turned[:, lanes]
                        mix_ref[odd, half, pl.ds(15 if odd else 0, 24, stride=HIGH), :] = border[
                            :, lanes
                        ]
                    turned = jnp.concatenate(
                        [mix_ref[odd, half, 0 : 17 * HIGH, :] for half in range(2)], axis=1
                    )
                    act = outside(act, HIGH, n, 1, 1, 34).astype(BF16)
                    turned = outside(turned, HIGH, n, 1, 1, 34).astype(BF16)
                    slot, beside = (1, 3) if odd else (2, 0)
                    for i in range(17):
                        rows = slice(i * HIGH, (i + 1) * HIGH)
                        at = (2 * (n + i) + a) * HIGH
                        s1_ref[at : at + HIGH, CH * slot : CH * slot + CH] = act[rows]
                        s1_ref[at : at + HIGH, CH * beside : CH * beside + CH] = turned[rows]
                        raw_ref[at : at + HIGH, CH * odd : CH * odd + CH] = value[rows]

                task(product, finish)

    for row, count in cuts(66, 6):
        for odd in range(2):

            def product(row=row, count=count, odd=odd):
                return conv(s1_ref, HIGH, row, count, 0 if odd else CH, w_high.at[0])

            def finish(value, row=row, count=count, odd=odd):
                act = activate(value, high_gain_ref[1:2, :])
                act = outside(act, HIGH, row, 1, 1, 66)
                slot, beside = (1, 3) if odd else (2, 0)
                rows = slice(row * HIGH, (row + count) * HIGH)
                s2_ref[rows, CH * slot : CH * slot + CH] = act.astype(BF16)
                s2_ref[rows, CH * beside : CH * beside + CH] = roll_rows(
                    act, -1 if odd else 1
                ).astype(BF16)

            task(product, finish, copies[6:7] if row == 0 and odd == 0 else None)

    turn = iota((256, 256), 0)
    turn = jnp.where(
        iota((256, 256), 1) == (turn % 16) * HIGH + turn // 16, 1.0, 0.0
    ).astype(BF16)
    outs = []
    late = []
    for n, row in enumerate(range(0, 64, 16)):
        for odd in range(2):

            def product(row=row, odd=odd):
                return conv(s2_ref, HIGH, row, 16, 0 if odd else CH, w_high.at[1])

            def finish(value, row=row, odd=odd):
                rows = slice((row + 2) * HIGH, (row + 18) * HIGH)
                value = value + raw_ref[rows, odd * CH : odd * CH + CH].astype(F32)
                done_ref[odd] = value.astype(BF16)

            def turned(odd=odd):
                return jnp.dot(turn, done_ref[odd], preferred_element_type=F32)

            def put(value, n=n, row=row, odd=odd):
                value = value.astype(BF16)
                for j in range(COLS):
                    at = (j + odd) * 16
                    out_ref[2 * j + odd, row : row + 16, :] = value[at : at + 16]
                if odd:
                    copy = pltpu.make_async_copy(
                        out_ref.at[:, row : row + 16], out_hbm.at[:, row : row + 16], out_sem.at[n]
                    )
                    copy.start()
                    outs.append(copy)

            task(product, finish, copies[7:8] if row == 0 and odd == 0 else None)
            late.append((turned, put))
            if len(late) > 1:
                task(*late.pop(0))
    task(*late.pop(0))

    before = None
    for number, (product, finish, wait) in enumerate(tasks):
        for copy in wait or ():
            copy.wait()
        value = product()
        if before is not None:
            before[0](before[1])
        before = (finish, value)
        if number == 5:
            copies[5].wait()
        if 5 <= number <= 8:
            phase_weights((number - 5) // 2, (number - 5) % 2)
    before[0](before[1])
    for copy in outs:
        copy.wait()


def shards(
    denoised_tokens,
    sequence_row_index,
    latent_frame_cache,
    cache_slot_order,
    temporal_taps_weight,
    input_weight,
    latent_conv_weights,
    upsampled_weight,
    upper_conv_weights,
    latent_norm_gains,
    upper_norm_gains,
):
    struct = jax.ShapeDtypeStruct
    vmem = pl.BlockSpec(memory_space=pltpu.VMEM)
    smem = pl.BlockSpec(memory_space=pltpu.SMEM)
    hbm = pl.BlockSpec(memory_space=pltpu.HBM)
    payload, own = pl.pallas_call(
        pack_kernel,
        in_specs=[smem, smem, vmem, vmem, vmem],
        out_specs=[vmem, vmem],
        out_shape=[struct((N_DEV, CHUNK, 128), BF16), struct((ROWS, 256), F32)],
        scratch_shapes=[pltpu.VMEM((72, 128), F32)],
        name="pack",
    )(
        sequence_row_index,
        cache_slot_order,
        denoised_tokens,
        latent_frame_cache,
        temporal_taps_weight,
    )
    arrived = lax.all_to_all(payload, ("lon", "band"), 0, 0, tiled=True)
    decoded = pl.pallas_call(
        block_kernel,
        in_specs=[hbm] * 9,
        out_specs=hbm,
        out_shape=struct((2 * COLS, 2 * ROWS, CH), BF16),
        scratch_shapes=[
            pltpu.VMEM((N_DEV, 8, 128), BF16),
            pltpu.VMEM((8, CHUNK, 128), BF16),
            pltpu.VMEM((ROWS, 256), F32),
            pltpu.VMEM((3, LAT, LAT), BF16),
            pltpu.VMEM((2, CH), F32),
            pltpu.VMEM((2, CH), F32),
            pltpu.VMEM((3, 128, CH), BF16),
            pltpu.VMEM((2, 3, 3 * CH, CH), BF16),
            pltpu.VMEM((9, CH, CH), BF16),
            pltpu.VMEM((2, 3, 3 * CH, CH), BF16),
            pltpu.VMEM((2, 2, 4 * CH, CH), BF16),
            pltpu.VMEM((N_DEV * 8, 128), F32),
            pltpu.VMEM((48 * LOW, 128), F32),
            pltpu.VMEM((40 * LOW, CH), F32),
            pltpu.VMEM((40 * LOW, 3 * CH), BF16),
            pltpu.VMEM((38 * LOW, 3 * CH), BF16),
            pltpu.VMEM((36 * HIGH, 2 * CH), BF16),
            pltpu.VMEM((2, 44 * LOW, 128), F32),
            pltpu.VMEM((68 * HIGH, 4 * CH), BF16),
            pltpu.VMEM((68 * HIGH, 2 * CH), BF16),
            pltpu.VMEM((66 * HIGH, 4 * CH), BF16),
            pltpu.VMEM((2, 2, 24 * HIGH, 128), F32),
            pltpu.VMEM((2, 256, CH), BF16),
            pltpu.VMEM((2 * COLS, 2 * ROWS, CH), BF16),
            pltpu.SemaphoreType.DMA((21,)),
            pltpu.SemaphoreType.DMA((4,)),
        ],
        compiler_params=pltpu.CompilerParams(vmem_limit_bytes=56 * 1024 * 1024),
        name="block",
    )(
        arrived,
        own,
        temporal_taps_weight,
        latent_norm_gains,
        upper_norm_gains,
        input_weight.reshape(3, 48, CH),
        latent_conv_weights.reshape(2, 3, 3 * CH, CH),
        upsampled_weight,
        upper_conv_weights.reshape(2, 3, 3 * CH, CH),
    )
    return decoded.transpose(1, 0, 2)


def solution(mesh):
    in_specs = (
        P("band", "lon", None),
        P("band", None),
        P(None, "band", "lon"),
        P(),
        P(),
        P(),
        P(),
        P(),
        P(),
        P(),
        P(),
    )
    out_specs = P("band", "lon", None)
    return jax.shard_map(shards, mesh=mesh, in_specs=in_specs, out_specs=out_specs, check_vma=False)
```

```python
import functools

import jax
import jax.numpy as jnp
from jax import lax
from jax.experimental import pallas as pl
from jax.experimental.pallas import tpu as pltpu
from jax.sharding import PartitionSpec as P

F32 = jnp.float32
BF16 = jnp.bfloat16

N_LON = 32
N_BAND = 4
ROWS = 32
COLS = 15
LAT = 16
CH = 256
HALO = 5
TOKEN = 480 * LAT
LANES = COLS * LAT
EDGE = HALO * LAT
WINDOW = LANES + 2 * EDGE
CHUNK = 24


def window_start(lon):
    return (LANES * lon - EDGE) // 128


def window_offset(lon):
    return (LANES * lon - EDGE) % 128


def iota(shape, dim):
    return lax.broadcasted_iota(jnp.int32, shape, dim)


def block_diagonal(tap):
    rows = jnp.where(iota((128, LAT), 0) % LAT == iota((128, LAT), 1), 1.0, 0.0).astype(BF16)
    cols = jnp.where(iota((LAT, 128), 1) % LAT == iota((LAT, 128), 0), 1.0, 0.0).astype(BF16)
    tall = jnp.dot(rows, tap, preferred_element_type=F32).astype(BF16)
    full = jnp.dot(tall, cols, preferred_element_type=F32)
    same = iota((128, 128), 0) // LAT == iota((128, 128), 1) // LAT
    return jnp.where(same, full, 0.0).astype(BF16)


def pack_kernel(index_ref, slot_ref, token_ref, cache_ref, taps_ref, send_ref, own_ref, x_ref):
    lon = lax.axis_index("lon")
    row = jnp.int32(0)
    for r in range(ROWS):
        row = jnp.where(index_ref[0, r] == lon, r, row)
    tag = row.astype(F32)
    for k in range(TOKEN // 128):
        piece = token_ref[0, :, 128 * k : 128 * k + 128].astype(F32)
        x_ref[k : k + 1, :] = piece
        if k < 4:
            x_ref[60 + k : 61 + k, :] = piece
    place = iota((8, 128), 0) * 128 + iota((8, 128), 1)
    for target in range(N_LON):
        start = window_start(target) % 60
        spot = (window_offset(target) + WINDOW) % 512
        tile = x_ref[start : start + 8, :]
        send_ref[target, 0:8, :] = jnp.where(place == spot, tag, tile).astype(BF16)

    diagonals = [block_diagonal(taps_ref[t]) for t in (1, 2)]
    mixed = jnp.zeros((2 * ROWS, 128), F32)
    for t in range(2):
        frame = cache_ref[slot_ref[t]]
        frame = jnp.concatenate([frame, jnp.zeros((ROWS, 256 - LANES), BF16)], axis=1)
        stacked = jnp.concatenate([frame[:, :128], frame[:, 128:]], axis=0)
        mixed = mixed + jnp.dot(stacked, diagonals[t], preferred_element_type=F32)
    own = jnp.concatenate([mixed[:ROWS], mixed[ROWS:]], axis=1)
    own_ref[...] = own

    for d_lon, v in ((-1, own[:, :EDGE]), (1, own[:, LANES - EDGE : LANES])):
        top = jnp.concatenate([v[:16, :], v[16:, : 128 - EDGE]], axis=1)
        low = jnp.concatenate(
            [v[16 + 4 * m : 20 + 4 * m, 128 - EDGE : EDGE] for m in range(4)], axis=1
        )
        full = jnp.concatenate([jnp.zeros((4, 128), F32), top, low], axis=0)
        to = lax.rem(lon + d_lon + N_LON, N_LON)
        first = send_ref[to, 0:8, :].astype(F32)
        send_ref[to, 0:8, :] = jnp.where(iota((8, 128), 0) < 4, first, full[:8]).astype(BF16)
        send_ref[to, 8:CHUNK, :] = full[8:].astype(BF16)


def mix_kernel(
    got_hbm,
    own_hbm,
    taps_hbm,
    out_ref,
    first_ref,
    last_ref,
    got_ref,
    near_ref,
    own_ref,
    taps_ref,
    tok_ref,
    sem,
):
    lon = lax.axis_index("lon")
    copies = [
        pltpu.make_async_copy(got_hbm.at[:, 0:8], got_ref, sem.at[0]),
        pltpu.make_async_copy(taps_hbm, taps_ref, sem.at[1]),
        pltpu.make_async_copy(own_hbm, own_ref, sem.at[2]),
    ]
    for n in range(2):
        source = lax.rem(lon + 2 * n - 1 + N_LON, N_LON)
        copies.append(pltpu.make_async_copy(got_hbm.at[source], near_ref.at[n], sem.at[3 + n]))
    for copy in copies:
        copy.start()
    for copy in copies:
        copy.wait()

    tok_ref[...] = got_ref[...].astype(F32).reshape(N_LON * 8, 128)
    x = jnp.concatenate([tok_ref[pl.ds(k, N_LON, stride=8), :] for k in range(4)], axis=1)
    offset = lax.rem(LANES * lon + (128 - EDGE), 128)
    x = pltpu.roll(x, lax.rem(512 - offset, 512), axis=1)
    tag = x[:, WINDOW : WINDOW + 1].astype(jnp.int32)
    select = jnp.where(tag == iota((N_LON, 128), 1), 1.0, 0.0)
    select = jnp.concatenate([select, jnp.zeros((128 - N_LON, 128), F32)], axis=0)
    select = select.T[:ROWS, :N_LON].astype(BF16)
    latent = jnp.dot(select, x.astype(BF16), preferred_element_type=F32).astype(BF16)

    def side(n):
        c = near_ref[n].astype(F32)[4:]
        low = jnp.concatenate([c[16:20, 32 * k : 32 * k + 32] for k in range(4)], axis=0)
        low = jnp.concatenate([c[:16, EDGE:], low], axis=1)
        return jnp.concatenate([c[:16, :EDGE], low], axis=0)

    cached = jnp.concatenate(
        [side(0), own_ref[:, :LANES], side(1), jnp.zeros((ROWS, 512 - WINDOW), F32)], axis=1
    )
    stacked = jnp.concatenate([latent[:, 128 * k : 128 * k + 128] for k in range(4)], axis=0)
    fresh = jnp.dot(stacked, block_diagonal(taps_ref[0]), preferred_element_type=F32)
    fresh = jnp.concatenate([fresh[ROWS * k : ROWS * k + ROWS] for k in range(4)], axis=1)
    temporal = jnp.where(iota((ROWS, 512), 1) < WINDOW, fresh + cached, 0.0)
    out_ref[...] = temporal.astype(BF16)
    first_ref[...] = temporal[:8].astype(BF16)
    last_ref[...] = temporal[ROWS - 8 :].astype(BF16)


def activate(values, gain):
    mean = jnp.sum(values * values, axis=-1, keepdims=True) * (1.0 / CH)
    half = values * lax.rsqrt(mean + 1e-06) * (0.5 * gain)
    return half * jnp.tanh(half) + half


def roll_rows(values, by):
    return pltpu.roll(values, by % values.shape[0], axis=0)


def cuts(rows, pieces):
    ends = [rows * k // pieces for k in range(pieces + 1)]
    return [(low, high - low) for low, high in zip(ends[:-1], ends[1:])]


LOW = 24
HIGH = 16


def block_kernel(
    temporal_hbm,
    above_hbm,
    below_hbm,
    low_gain_hbm,
    high_gain_hbm,
    w_in_hbm,
    w_low_hbm,
    w_up_hbm,
    w_high_hbm,
    out_hbm,
    temporal_ref,
    rim_ref,
    low_gain_ref,
    high_gain_ref,
    w_in,
    w_low,
    w_up,
    w_high,
    w_phase,
    u_ref,
    open_ref,
    a1_ref,
    a2_ref,
    low_ref,
    lowf_ref,
    s1_ref,
    raw_ref,
    s2_ref,
    mix_ref,
    out_ref,
    in_sem,
    out_sem,
):
    band = lax.axis_index("band")
    copies = [pltpu.make_async_copy(w_in_hbm.at[p], w_in.at[p, 0:48], in_sem.at[p]) for p in range(3)]
    copies.append(pltpu.make_async_copy(w_low_hbm.at[0], w_low.at[0], in_sem.at[3]))
    copies.append(pltpu.make_async_copy(w_low_hbm.at[1], w_low.at[1], in_sem.at[4]))
    copies.append(pltpu.make_async_copy(w_up_hbm, w_up, in_sem.at[5]))
    copies.append(pltpu.make_async_copy(w_high_hbm.at[0], w_high.at[0], in_sem.at[6]))
    copies.append(pltpu.make_async_copy(w_high_hbm.at[1], w_high.at[1], in_sem.at[7]))
    small = [
        pltpu.make_async_copy(source, target, in_sem.at[8 + n])
        for n, (source, target) in enumerate(
            (
                (temporal_hbm, temporal_ref),
                (above_hbm, rim_ref.at[0]),
                (below_hbm, rim_ref.at[1]),
                (low_gain_hbm, low_gain_ref),
                (high_gain_hbm, high_gain_ref),
            )
        )
    ]
    for copy in small + copies:
        copy.start()
    w_in[:, 48:128, :] = jnp.zeros((3, 80, CH), BF16)

    for copy in small:
        copy.wait()
    above = jnp.where(band > 0, rim_ref[0].astype(F32), 0.0)
    below = jnp.where(band < N_BAND - 1, rim_ref[1].astype(F32), 0.0)
    temporal = jnp.concatenate(
        [
            above[8 - HALO :],
            temporal_ref[...].astype(F32),
            below[:HALO],
            jnp.zeros((6, 512), F32),
        ],
        axis=0,
    )

    wide = jnp.concatenate([temporal, jnp.zeros((48, 128), F32)], axis=1)
    for j in range(LOW):
        piece = wide[:, 128 * (j // 8) : 128 * (j // 8) + 256]
        turn = LAT * (j % 8)
        if turn:
            piece = pltpu.roll(piece, 256 - turn, axis=1)
        u_ref[pl.ds(j, 48, stride=LOW), :] = piece[:, :128]

    def outside(value, pitch, row, top, bottom, rows):
        count = value.shape[0] // pitch
        above = min(max(top - row, 0), count)
        below = min(max(row + count - (rows - bottom), 0), count)
        parts = []
        if above:
            parts.append(jnp.where(band == 0, 0.0, value[: above * pitch]))
        parts.append(value[above * pitch : (count - below) * pitch])
        if below:
            parts.append(jnp.where(band == N_BAND - 1, 0.0, value[(count - below) * pitch :]))
        return parts[0] if len(parts) == 1 else jnp.concatenate(parts, axis=0)

    def conv(ref, pitch, row, count, lane, weight):
        total = None
        for p in range(3):
            part = jnp.dot(
                ref[(row + p) * pitch : (row + p + count) * pitch, lane : lane + 3 * CH],
                weight[p],
                preferred_element_type=F32,
            )
            total = part if total is None else total + part
        return total

    def spread(act, ref, row):
        rows = slice(row * LOW, row * LOW + act.shape[0])
        ref[rows, 0:CH] = roll_rows(act, 1).astype(BF16)
        ref[rows, CH : 2 * CH] = act.astype(BF16)
        ref[rows, 2 * CH :] = roll_rows(act, -1).astype(BF16)

    tasks = []

    def task(product, finish, wait=None):
        tasks.append((product, finish, wait))

    for row, count in cuts(40, 3):

        def product(row=row, count=count):
            lhs = [u_ref[(row + p) * LOW : (row + p + count) * LOW, :] for p in range(3)]
            lhs = jnp.concatenate(lhs, axis=1).astype(BF16)
            return jnp.dot(lhs, w_in[...].reshape(384, CH), preferred_element_type=F32)

        def finish(value, row=row, count=count):
            value = value.astype(BF16).astype(F32)
            open_ref[row * LOW : (row + count) * LOW, :] = value
            act = activate(value, low_gain_ref[0:1, :])
            spread(outside(act, LOW, row, 4, 4, 40), a1_ref, row)

        task(product, finish, copies[:3] if row == 0 else None)

    for row, count in cuts(38, 3):

        def product(row=row, count=count):
            return conv(a1_ref, LOW, row, count, 0, w_low.at[0])

        def finish(value, row=row):
            act = activate(value, low_gain_ref[1:2, :])
            spread(outside(act, LOW, row, 3, 3, 38), a2_ref, row)

        task(product, finish, copies[3:4] if row == 0 else None)

    for row, count in cuts(36, 3):

        def product(row=row, count=count):
            return conv(a2_ref, LOW, row, count, 0, w_low.at[1])

        def finish(value, row=row, count=count):
            low = open_ref[(row + 2) * LOW : (row + 2 + count) * LOW, :] + value
            low = outside(low.astype(BF16).astype(F32), LOW, row, 2, 2, 36)
            for half in range(2):
                lowf_ref[half, row * LOW : (row + count) * LOW, :] = low[
                    :, 128 * half : 128 * half + 128
                ]
            for k in range(2):
                part = roll_rows(low, -(3 + k)).reshape(count, LOW, CH)[:, :HIGH]
                low_ref[row * HIGH : (row + count) * HIGH, CH * k : CH * k + CH] = part.reshape(
                    count * HIGH, CH
                ).astype(BF16)

        task(product, finish, copies[4:5] if row == 0 else None)

    def phase_weights(a, odd):
        for r in range(2):
            taps = ((0,), (1, 2)) if a == 0 else ((0, 1), (2,))
            sides = ((0, 1), (2,)) if odd else ((0,), (1, 2))
            for c in range(2):
                total = None
                for p in taps[r]:
                    for q in sides[c]:
                        one = w_up[3 * p + q].astype(F32)
                        total = one if total is None else total + one
                at = (2 * r + c) * CH
                w_phase[a, odd, at : at + CH, :] = total.astype(BF16)

    for n in (0, 17):
        for a in range(2):
            for odd in range(2):

                def product(n=n, a=a, odd=odd):
                    parts = []
                    for r in range(2):
                        at = n + a + r
                        col = 19 if odd else 2
                        pair = [
                            lowf_ref[half, pl.ds(at * LOW + col + c, 24, stride=LOW), :]
                            for c in range(2)
                            for half in range(2)
                        ]
                        pair = jnp.concatenate(pair, axis=1).astype(BF16)
                        main = low_ref[at * HIGH : (at + 17) * HIGH, :]
                        pad = jnp.zeros((8, 2 * CH), BF16)
                        parts.append(jnp.concatenate([main, pair, pad], axis=0))
                    return jnp.dot(
                        jnp.concatenate(parts, axis=1),
                        w_phase[a, odd],
                        preferred_element_type=F32,
                    )

                def finish(value, n=n, a=a, odd=odd):
                    value = value[: 17 * HIGH + 24].astype(BF16)
                    act = activate(value.astype(F32), high_gain_ref[0:1, :])
                    border = act[17 * HIGH :]
                    act = act[: 17 * HIGH]
                    turned = roll_rows(act, -1 if odd else 1)
                    for half in range(2):
                        lanes = slice(128 * half, 128 * half + 128)
                        mix_ref[odd, half, 0 : 17 * HIGH, :] = turned[:, lanes]
                        mix_ref[odd, half, pl.ds(15 if odd else 0, 24, stride=HIGH), :] = border[
                            :, lanes
                        ]
                    turned = jnp.concatenate(
                        [mix_ref[odd, half, 0 : 17 * HIGH, :] for half in range(2)], axis=1
                    )
                    act = outside(act, HIGH, n, 1, 1, 34).astype(BF16)
                    turned = outside(turned, HIGH, n, 1, 1, 34).astype(BF16)
                    slot, beside = (1, 3) if odd else (2, 0)
                    for i in range(17):
                        rows = slice(i * HIGH, (i + 1) * HIGH)
                        at = (2 * (n + i) + a) * HIGH
                        s1_ref[at : at + HIGH, CH * slot : CH * slot + CH] = act[rows]
                        s1_ref[at : at + HIGH, CH * beside : CH * beside + CH] = turned[rows]
                        raw_ref[at : at + HIGH, CH * odd : CH * odd + CH] = value[rows]

                task(product, finish)

    for row, count in cuts(66, 6):
        for odd in range(2):

            def product(row=row, count=count, odd=odd):
                return conv(s1_ref, HIGH, row, count, 0 if odd else CH, w_high.at[0])

            def finish(value, row=row, count=count, odd=odd):
                act = activate(value, high_gain_ref[1:2, :])
                act = outside(act, HIGH, row, 1, 1, 66)
                slot, beside = (1, 3) if odd else (2, 0)
                rows = slice(row * HIGH, (row + count) * HIGH)
                s2_ref[rows, CH * slot : CH * slot + CH] = act.astype(BF16)
                s2_ref[rows, CH * beside : CH * beside + CH] = roll_rows(
                    act, -1 if odd else 1
                ).astype(BF16)

            task(product, finish, copies[6:7] if row == 0 and odd == 0 else None)

    outs = []
    for n, row in enumerate(range(0, 64, 16)):
        for odd in range(2):

            def product(row=row, odd=odd):
                return conv(s2_ref, HIGH, row, 16, 0 if odd else CH, w_high.at[1])

            def finish(value, n=n, row=row, odd=odd):
                rows = slice((row + 2) * HIGH, (row + 18) * HIGH)
                value = value + raw_ref[rows, odd * CH : odd * CH + CH].astype(F32)
                value = jnp.swapaxes(value.reshape(16, HIGH, CH), 0, 1).astype(BF16)
                for j in range(COLS):
                    out_ref[2 * j + odd, row : row + 16, :] = value[j + odd]
                if odd:
                    copy = pltpu.make_async_copy(
                        out_ref.at[:, row : row + 16], out_hbm.at[:, row : row + 16], out_sem.at[n]
                    )
                    copy.start()
                    outs.append(copy)

            task(product, finish, copies[7:8] if row == 0 and odd == 0 else None)

    before = None
    for number, (product, finish, wait) in enumerate(tasks):
        for copy in wait or ():
            copy.wait()
        value = product()
        if before is not None:
            before[0](before[1])
        before = (finish, value)
        if number == 4:
            copies[5].wait()
        if 4 <= number <= 7:
            phase_weights((number - 4) // 2, (number - 4) % 2)
    before[0](before[1])
    for copy in outs:
        copy.wait()


def shards(
    denoised_tokens,
    sequence_row_index,
    latent_frame_cache,
    cache_slot_order,
    temporal_taps_weight,
    input_weight,
    latent_conv_weights,
    upsampled_weight,
    upper_conv_weights,
    latent_norm_gains,
    upper_norm_gains,
):
    struct = jax.ShapeDtypeStruct
    vmem = pl.BlockSpec(memory_space=pltpu.VMEM)
    smem = pl.BlockSpec(memory_space=pltpu.SMEM)
    hbm = pl.BlockSpec(memory_space=pltpu.HBM)
    anywhere = pl.BlockSpec(memory_space=pl.ANY)
    payload, own = pl.pallas_call(
        pack_kernel,
        in_specs=[smem, smem, vmem, vmem, vmem],
        out_specs=[vmem, vmem],
        out_shape=[struct((N_LON, CHUNK, 128), BF16), struct((ROWS, 256), F32)],
        scratch_shapes=[pltpu.VMEM((72, 128), F32)],
        name="pack",
    )(
        sequence_row_index,
        cache_slot_order,
        denoised_tokens,
        latent_frame_cache,
        temporal_taps_weight,
    )
    arrived = lax.all_to_all(payload, "lon", 0, 0, tiled=True)
    temporal, first, last = pl.pallas_call(
        mix_kernel,
        in_specs=[hbm] * 3,
        out_specs=[vmem] * 3,
        out_shape=[struct((ROWS, 512), BF16), struct((8, 512), BF16), struct((8, 512), BF16)],
        scratch_shapes=[
            pltpu.VMEM((N_LON, 8, 128), BF16),
            pltpu.VMEM((2, CHUNK, 128), BF16),
            pltpu.VMEM((ROWS, 256), F32),
            pltpu.VMEM((3, LAT, LAT), BF16),
            pltpu.VMEM((N_LON * 8, 128), F32),
            pltpu.SemaphoreType.DMA((5,)),
        ],
        compiler_params=pltpu.CompilerParams(vmem_limit_bytes=56 * 1024 * 1024),
        name="mix",
    )(arrived, own, temporal_taps_weight)
    ring = [(b, (b + 1) % N_BAND) for b in range(N_BAND)]
    above = lax.ppermute(last, "band", ring)
    below = lax.ppermute(first, "band", [(b, a) for a, b in ring])
    decoded = pl.pallas_call(
        block_kernel,
        in_specs=[anywhere] * 3 + [hbm] * 6,
        out_specs=hbm,
        out_shape=struct((2 * COLS, 2 * ROWS, CH), BF16),
        scratch_shapes=[
            pltpu.VMEM((ROWS, 512), BF16),
            pltpu.VMEM((2, 8, 512), BF16),
            pltpu.VMEM((2, CH), F32),
            pltpu.VMEM((2, CH), F32),
            pltpu.VMEM((3, 128, CH), BF16),
            pltpu.VMEM((2, 3, 3 * CH, CH), BF16),
            pltpu.VMEM((9, CH, CH), BF16),
            pltpu.VMEM((2, 3, 3 * CH, CH), BF16),
            pltpu.VMEM((2, 2, 4 * CH, CH), BF16),
            pltpu.VMEM((48 * LOW, 128), F32),
            pltpu.VMEM((40 * LOW, CH), F32),
            pltpu.VMEM((40 * LOW, 3 * CH), BF16),
            pltpu.VMEM((38 * LOW, 3 * CH), BF16),
            pltpu.VMEM((36 * HIGH, 2 * CH), BF16),
            pltpu.VMEM((2, 44 * LOW, 128), F32),
            pltpu.VMEM((68 * HIGH, 4 * CH), BF16),
            pltpu.VMEM((68 * HIGH, 2 * CH), BF16),
            pltpu.VMEM((66 * HIGH, 4 * CH), BF16),
            pltpu.VMEM((2, 2, 24 * HIGH, 128), F32),
            pltpu.VMEM((2 * COLS, 2 * ROWS, CH), BF16),
            pltpu.SemaphoreType.DMA((13,)),
            pltpu.SemaphoreType.DMA((4,)),
        ],
        compiler_params=pltpu.CompilerParams(vmem_limit_bytes=56 * 1024 * 1024),
        name="block",
    )(
        temporal,
        above,
        below,
        latent_norm_gains,
        upper_norm_gains,
        input_weight.reshape(3, 48, CH),
        latent_conv_weights.reshape(2, 3, 3 * CH, CH),
        upsampled_weight,
        upper_conv_weights.reshape(2, 3, 3 * CH, CH),
    )
    return decoded.transpose(1, 0, 2)


def solution(mesh):
    in_specs = (
        P("band", "lon", None),
        P("band", None),
        P(None, "band", "lon"),
        P(),
        P(),
        P(),
        P(),
        P(),
        P(),
        P(),
        P(),
    )
    out_specs = P("band", "lon", None)
    return jax.shard_map(shards, mesh=mesh, in_specs=in_specs, out_specs=out_specs, check_vma=False)
```

```python
import functools

import jax
import jax.numpy as jnp
from jax import lax
from jax.experimental import pallas as pl
from jax.experimental.pallas import tpu as pltpu
from jax.sharding import PartitionSpec as P

F32 = jnp.float32
BF16 = jnp.bfloat16

N_LON = 32
N_BAND = 4
ROWS = 32
COLS = 15
LAT = 16
CH = 256
HALO = 5
TOKEN = 480 * LAT
LANES = COLS * LAT
EDGE = HALO * LAT
WINDOW = LANES + 2 * EDGE
CHUNK = 24


def window_start(lon):
    return (LANES * lon - EDGE) // 128


def window_offset(lon):
    return (LANES * lon - EDGE) % 128


def iota(shape, dim):
    return lax.broadcasted_iota(jnp.int32, shape, dim)


def block_diagonal(tap):
    rows = jnp.where(iota((128, LAT), 0) % LAT == iota((128, LAT), 1), 1.0, 0.0).astype(BF16)
    cols = jnp.where(iota((LAT, 128), 1) % LAT == iota((LAT, 128), 0), 1.0, 0.0).astype(BF16)
    tall = jnp.dot(rows, tap, preferred_element_type=F32).astype(BF16)
    full = jnp.dot(tall, cols, preferred_element_type=F32)
    same = iota((128, 128), 0) // LAT == iota((128, 128), 1) // LAT
    return jnp.where(same, full, 0.0).astype(BF16)


def pack_kernel(index_ref, slot_ref, token_ref, cache_ref, taps_ref, send_ref, own_ref, x_ref):
    lon = lax.axis_index("lon")
    row = jnp.int32(0)
    for r in range(ROWS):
        row = jnp.where(index_ref[0, r] == lon, r, row)
    tag = row.astype(F32)
    for k in range(TOKEN // 128):
        piece = token_ref[0, :, 128 * k : 128 * k + 128].astype(F32)
        x_ref[k : k + 1, :] = piece
        if k < 4:
            x_ref[60 + k : 61 + k, :] = piece
    place = iota((8, 128), 0) * 128 + iota((8, 128), 1)
    for target in range(N_LON):
        start = window_start(target) % 60
        spot = (window_offset(target) + WINDOW) % 512
        tile = x_ref[start : start + 8, :]
        send_ref[target, 0:8, :] = jnp.where(place == spot, tag, tile).astype(BF16)

    diagonals = [block_diagonal(taps_ref[t]) for t in (1, 2)]
    mixed = jnp.zeros((2 * ROWS, 128), F32)
    for t in range(2):
        frame = cache_ref[slot_ref[t]]
        frame = jnp.concatenate([frame, jnp.zeros((ROWS, 256 - LANES), BF16)], axis=1)
        stacked = jnp.concatenate([frame[:, :128], frame[:, 128:]], axis=0)
        mixed = mixed + jnp.dot(stacked, diagonals[t], preferred_element_type=F32)
    own = jnp.concatenate([mixed[:ROWS], mixed[ROWS:]], axis=1)
    own_ref[...] = own

    for d_lon, v in ((-1, own[:, :EDGE]), (1, own[:, LANES - EDGE : LANES])):
        top = jnp.concatenate([v[:16, :], v[16:, : 128 - EDGE]], axis=1)
        low = jnp.concatenate(
            [v[16 + 4 * m : 20 + 4 * m, 128 - EDGE : EDGE] for m in range(4)], axis=1
        )
        full = jnp.concatenate([jnp.zeros((4, 128), F32), top, low], axis=0)
        to = lax.rem(lon + d_lon + N_LON, N_LON)
        first = send_ref[to, 0:8, :].astype(F32)
        send_ref[to, 0:8, :] = jnp.where(iota((8, 128), 0) < 4, first, full[:8]).astype(BF16)
        send_ref[to, 8:CHUNK, :] = full[8:].astype(BF16)


def mix_kernel(
    got_hbm,
    own_hbm,
    taps_hbm,
    out_ref,
    first_ref,
    last_ref,
    got_ref,
    near_ref,
    own_ref,
    taps_ref,
    tok_ref,
    sem,
):
    lon = lax.axis_index("lon")
    copies = [
        pltpu.make_async_copy(got_hbm.at[:, 0:8], got_ref, sem.at[0]),
        pltpu.make_async_copy(taps_hbm, taps_ref, sem.at[1]),
        pltpu.make_async_copy(own_hbm, own_ref, sem.at[2]),
    ]
    for n in range(2):
        source = lax.rem(lon + 2 * n - 1 + N_LON, N_LON)
        copies.append(pltpu.make_async_copy(got_hbm.at[source], near_ref.at[n], sem.at[3 + n]))
    for copy in copies:
        copy.start()
    for copy in copies:
        copy.wait()

    tok_ref[...] = got_ref[...].astype(F32).reshape(N_LON * 8, 128)
    x = jnp.concatenate([tok_ref[pl.ds(k, N_LON, stride=8), :] for k in range(4)], axis=1)
    offset = lax.rem(LANES * lon + (128 - EDGE), 128)
    x = pltpu.roll(x, lax.rem(512 - offset, 512), axis=1)
    tag = x[:, WINDOW : WINDOW + 1].astype(jnp.int32)
    select = jnp.where(tag == iota((N_LON, 128), 1), 1.0, 0.0)
    select = jnp.concatenate([select, jnp.zeros((128 - N_LON, 128), F32)], axis=0)
    select = select.T[:ROWS, :N_LON].astype(BF16)
    latent = jnp.dot(select, x.astype(BF16), preferred_element_type=F32).astype(BF16)

    def side(n):
        c = near_ref[n].astype(F32)[4:]
        low = jnp.concatenate([c[16:20, 32 * k : 32 * k + 32] for k in range(4)], axis=0)
        low = jnp.concatenate([c[:16, EDGE:], low], axis=1)
        return jnp.concatenate([c[:16, :EDGE], low], axis=0)

    cached = jnp.concatenate(
        [side(0), own_ref[:, :LANES], side(1), jnp.zeros((ROWS, 512 - WINDOW), F32)], axis=1
    )
    stacked = jnp.concatenate([latent[:, 128 * k : 128 * k + 128] for k in range(4)], axis=0)
    fresh = jnp.dot(stacked, block_diagonal(taps_ref[0]), preferred_element_type=F32)
    fresh = jnp.concatenate([fresh[ROWS * k : ROWS * k + ROWS] for k in range(4)], axis=1)
    temporal = jnp.where(iota((ROWS, 512), 1) < WINDOW, fresh + cached, 0.0)
    out_ref[...] = temporal.astype(BF16)
    first_ref[...] = temporal[:8].astype(BF16)
    last_ref[...] = temporal[ROWS - 8 :].astype(BF16)


def activate(values, gain):
    mean = jnp.sum(values * values, axis=-1, keepdims=True) * (1.0 / CH)
    half = values * lax.rsqrt(mean + 1e-06) * (0.5 * gain)
    return half * jnp.tanh(half) + half


def roll_rows(values, by):
    return pltpu.roll(values, by % values.shape[0], axis=0)


def cuts(rows, pieces):
    ends = [rows * k // pieces for k in range(pieces + 1)]
    return [(low, high - low) for low, high in zip(ends[:-1], ends[1:])]


LOW = 24
HIGH = 16


def block_kernel(
    temporal_hbm,
    above_hbm,
    below_hbm,
    low_gain_hbm,
    high_gain_hbm,
    w_in_hbm,
    w_low_hbm,
    w_up_hbm,
    w_high_hbm,
    out_hbm,
    temporal_ref,
    rim_ref,
    low_gain_ref,
    high_gain_ref,
    w_in,
    w_low,
    w_up,
    w_phase,
    w_high,
    w_mid,
    u_ref,
    open_ref,
    a1_ref,
    a2_ref,
    low_ref,
    lowf_ref,
    s1_ref,
    raw_ref,
    s2_ref,
    mix_ref,
    out_ref,
    in_sem,
    out_sem,
):
    band = lax.axis_index("band")
    copies = [pltpu.make_async_copy(w_in_hbm.at[p], w_in.at[p, 0:48], in_sem.at[p]) for p in range(3)]
    copies.append(pltpu.make_async_copy(w_low_hbm.at[0], w_low.at[0], in_sem.at[3]))
    copies.append(pltpu.make_async_copy(w_low_hbm.at[1], w_low.at[1], in_sem.at[4]))
    copies.append(pltpu.make_async_copy(w_up_hbm, w_up, in_sem.at[5]))
    for n in range(2):
        for k in range(3):
            target = w_mid.at[n] if k == 1 else w_high.at[n, k // 2 * 3]
            pair = (w_high_hbm.at[n, :, k], target)
            copies.append(pltpu.make_async_copy(*pair, in_sem.at[6 + 3 * n + k]))
    small = [
        pltpu.make_async_copy(source, target, in_sem.at[12 + n])
        for n, (source, target) in enumerate(
            (
                (temporal_hbm, temporal_ref),
                (above_hbm, rim_ref.at[0]),
                (below_hbm, rim_ref.at[1]),
                (low_gain_hbm, low_gain_ref),
                (high_gain_hbm, high_gain_ref),
            )
        )
    ]
    for copy in small + copies:
        copy.start()
    w_in[:, 48:128, :] = jnp.zeros((3, 80, CH), BF16)

    for copy in small:
        copy.wait()
    above = jnp.where(band > 0, rim_ref[0].astype(F32), 0.0)
    below = jnp.where(band < N_BAND - 1, rim_ref[1].astype(F32), 0.0)
    temporal = jnp.concatenate(
        [
            above[8 - HALO :],
            temporal_ref[...].astype(F32),
            below[:HALO],
            jnp.zeros((6, 512), F32),
        ],
        axis=0,
    )

    wide = jnp.concatenate([temporal, jnp.zeros((48, 128), F32)], axis=1)
    for j in range(LOW):
        piece = wide[:, 128 * (j // 8) : 128 * (j // 8) + 256]
        turn = LAT * (j % 8)
        if turn:
            piece = pltpu.roll(piece, 256 - turn, axis=1)
        u_ref[pl.ds(j, 48, stride=LOW), :] = piece[:, :128]

    def outside(value, pitch, row, top, bottom, rows):
        count = value.shape[0] // pitch
        above = min(max(top - row, 0), count)
        below = min(max(row + count - (rows - bottom), 0), count)
        parts = []
        if above:
            parts.append(jnp.where(band == 0, 0.0, value[: above * pitch]))
        parts.append(value[above * pitch : (count - below) * pitch])
        if below:
            parts.append(jnp.where(band == N_BAND - 1, 0.0, value[(count - below) * pitch :]))
        return parts[0] if len(parts) == 1 else jnp.concatenate(parts, axis=0)

    def conv(ref, pitch, row, count, lane, weight):
        total = None
        for p in range(3):
            part = jnp.dot(
                ref[(row + p) * pitch : (row + p + count) * pitch, lane : lane + 3 * CH],
                weight[p],
                preferred_element_type=F32,
            )
            total = part if total is None else total + part
        return total

    def spread(act, ref, row):
        rows = slice(row * LOW, row * LOW + act.shape[0])
        ref[rows, 0:CH] = roll_rows(act, 1).astype(BF16)
        ref[rows, CH : 2 * CH] = act.astype(BF16)
        ref[rows, 2 * CH :] = roll_rows(act, -1).astype(BF16)

    tasks = []

    def task(product, finish, wait=None):
        tasks.append((product, finish, wait))

    for row, count in cuts(40, 3):

        def product(row=row, count=count):
            lhs = [u_ref[(row + p) * LOW : (row + p + count) * LOW, :] for p in range(3)]
            lhs = jnp.concatenate(lhs, axis=1).astype(BF16)
            return jnp.dot(lhs, w_in[...].reshape(384, CH), preferred_element_type=F32)

        def finish(value, row=row, count=count):
            value = value.astype(BF16).astype(F32)
            open_ref[row * LOW : (row + count) * LOW, :] = value
            act = activate(value, low_gain_ref[0:1, :])
            spread(outside(act, LOW, row, 4, 4, 40), a1_ref, row)

        task(product, finish, copies[:3] if row == 0 else None)

    for row, count in cuts(38, 3):

        def product(row=row, count=count):
            return conv(a1_ref, LOW, row, count, 0, w_low.at[0])

        def finish(value, row=row):
            act = activate(value, low_gain_ref[1:2, :])
            spread(outside(act, LOW, row, 3, 3, 38), a2_ref, row)

        task(product, finish, copies[3:4] if row == 0 else None)

    for row, count in cuts(36, 3):

        def product(row=row, count=count):
            return conv(a2_ref, LOW, row, count, 0, w_low.at[1])

        def finish(value, row=row, count=count):
            low = open_ref[(row + 2) * LOW : (row + 2 + count) * LOW, :] + value
            low = outside(low.astype(BF16).astype(F32), LOW, row, 2, 2, 36)
            for half in range(2):
                lowf_ref[half, row * LOW : (row + count) * LOW, :] = low[
                    :, 128 * half : 128 * half + 128
                ]
            for k in range(2):
                part = roll_rows(low, -(3 + k)).reshape(count, LOW, CH)[:, :HIGH]
                low_ref[row * HIGH : (row + count) * HIGH, CH * k : CH * k + CH] = part.reshape(
                    count * HIGH, CH
                ).astype(BF16)

        task(product, finish, copies[4:5] if row == 0 else None)

    def phase_weights(a, odd):
        for r in range(2):
            taps = ((0,), (1, 2)) if a == 0 else ((0, 1), (2,))
            sides = ((0, 1), (2,)) if odd else ((0,), (1, 2))
            for c in range(2):
                total = None
                for p in taps[r]:
                    for q in sides[c]:
                        one = w_up[3 * p + q].astype(F32)
                        total = one if total is None else total + one
                at = (2 * r + c) * CH
                w_phase[a, odd, at : at + CH, :] = total.astype(BF16)

    def sum_weights(n, p):
        outer = w_high[n, 0, p].astype(F32) + w_high[n, 3, p].astype(F32)
        inner = w_mid[n, p].astype(F32)
        w_high[n, 1, p] = (0.5 * (outer + inner)).astype(BF16)
        w_high[n, 2, p] = (0.5 * (outer - inner)).astype(BF16)

    beside = {}
    for k in range(4):
        beside[3 + k] = (copies[5:6] if k == 0 else (), phase_weights, (k // 2, k % 2))
    for p in range(3):
        beside[7 + p] = (copies[6:9] if p == 0 else (), sum_weights, (0, p))
        beside[17 + p] = (copies[9:12] if p == 0 else (), sum_weights, (1, p))

    held = []

    def quads(evens, odd, odd_next):
        even_last, even = evens
        parts = (even_last - even, odd + even, even - odd, odd - odd_next)
        return [part.astype(BF16) for part in parts]

    def pairs(ref, row, count, weight):
        m = []
        for k in range(4):
            total = None
            for p in range(3):
                part = jnp.dot(
                    ref[(row + p) * HIGH : (row + p + count) * HIGH, CH * k : CH * k + CH],
                    weight[k, p],
                    preferred_element_type=F32,
                )
                total = part if total is None else total + part
            m.append(total)
        return m[0] + m[1] + m[2], m[1] - m[2] - m[3]

    for n in (0, 17):
        for a in range(2):
            for odd in range(2):

                def product(n=n, a=a, odd=odd):
                    parts = []
                    for r in range(2):
                        at = n + a + r
                        col = 19 if odd else 2
                        pair = [
                            lowf_ref[half, pl.ds(at * LOW + col + c, 24, stride=LOW), :]
                            for c in range(2)
                            for half in range(2)
                        ]
                        pair = jnp.concatenate(pair, axis=1).astype(BF16)
                        main = low_ref[at * HIGH : (at + 17) * HIGH, :]
                        pad = jnp.zeros((8, 2 * CH), BF16)
                        parts.append(jnp.concatenate([main, pair, pad], axis=0))
                    return jnp.dot(
                        jnp.concatenate(parts, axis=1),
                        w_phase[a, odd],
                        preferred_element_type=F32,
                    )

                def finish(value, n=n, a=a, odd=odd):
                    value = value[: 17 * HIGH + 24].astype(BF16)
                    act = activate(value.astype(F32), high_gain_ref[0:1, :])
                    border = act[17 * HIGH :]
                    act = act[: 17 * HIGH]
                    turned = roll_rows(act, -1 if odd else 1)
                    for half in range(2):
                        lanes = slice(128 * half, 128 * half + 128)
                        mix_ref[odd, half, 0 : 17 * HIGH, :] = turned[:, lanes]
                        mix_ref[odd, half, pl.ds(15 if odd else 0, 24, stride=HIGH), :] = border[
                            :, lanes
                        ]
                    turned = jnp.concatenate(
                        [mix_ref[odd, half, 0 : 17 * HIGH, :] for half in range(2)], axis=1
                    )
                    act = outside(act, HIGH, n, 1, 1, 34)
                    turned = outside(turned, HIGH, n, 1, 1, 34)
                    if odd:
                        parts = quads(held.pop(), act, turned)
                    else:
                        held.append((turned, act))
                    for i in range(17):
                        rows = slice(i * HIGH, (i + 1) * HIGH)
                        at = (2 * (n + i) + a) * HIGH
                        if odd:
                            for k in range(4):
                                s1_ref[at : at + HIGH, CH * k : CH * k + CH] = parts[k][rows]
                        raw_ref[at : at + HIGH, CH * odd : CH * odd + CH] = value[rows]

                task(product, finish)

    for row, count in cuts(66, 6):

        def product(row=row, count=count):
            return pairs(s1_ref, row, count, w_high.at[0])

        def finish(values, row=row, count=count):
            odd, even = (
                outside(activate(value, high_gain_ref[1:2, :]), HIGH, row, 1, 1, 66)
                for value in values
            )
            parts = quads((roll_rows(even, 1), even), odd, roll_rows(odd, -1))
            for k in range(4):
                s2_ref[row * HIGH : (row + count) * HIGH, CH * k : CH * k + CH] = parts[k]

        task(product, finish)

    outs = []
    for n, row in enumerate(range(0, 64, 16)):

        def product(row=row):
            return pairs(s2_ref, row, 16, w_high.at[1])

        def finish(values, n=n, row=row):
            rows = slice((row + 2) * HIGH, (row + 18) * HIGH)
            for odd in range(2):
                value = values[1 - odd] + raw_ref[rows, odd * CH : odd * CH + CH].astype(F32)
                value = jnp.swapaxes(value.reshape(16, HIGH, CH), 0, 1).astype(BF16)
                for j in range(COLS):
                    out_ref[2 * j + odd, row : row + 16, :] = value[j + odd]
            copy = pltpu.make_async_copy(
                out_ref.at[:, row : row + 16], out_hbm.at[:, row : row + 16], out_sem.at[n]
            )
            copy.start()
            outs.append(copy)

        task(product, finish)

    before = None
    for number, (product, finish, wait) in enumerate(tasks):
        for copy in wait or ():
            copy.wait()
        value = product()
        if before is not None:
            before[0](before[1])
        before = (finish, value)
        if number in beside:
            arrive, work, which = beside[number]
            for copy in arrive:
                copy.wait()
            work(*which)
    before[0](before[1])
    for copy in outs:
        copy.wait()


def shards(
    denoised_tokens,
    sequence_row_index,
    latent_frame_cache,
    cache_slot_order,
    temporal_taps_weight,
    input_weight,
    latent_conv_weights,
    upsampled_weight,
    upper_conv_weights,
    latent_norm_gains,
    upper_norm_gains,
):
    struct = jax.ShapeDtypeStruct
    vmem = pl.BlockSpec(memory_space=pltpu.VMEM)
    smem = pl.BlockSpec(memory_space=pltpu.SMEM)
    hbm = pl.BlockSpec(memory_space=pltpu.HBM)
    anywhere = pl.BlockSpec(memory_space=pl.ANY)
    payload, own = pl.pallas_call(
        pack_kernel,
        in_specs=[smem, smem, vmem, vmem, vmem],
        out_specs=[vmem, vmem],
        out_shape=[struct((N_LON, CHUNK, 128), BF16), struct((ROWS, 256), F32)],
        scratch_shapes=[pltpu.VMEM((72, 128), F32)],
        name="pack",
    )(
        sequence_row_index,
        cache_slot_order,
        denoised_tokens,
        latent_frame_cache,
        temporal_taps_weight,
    )
    arrived = lax.all_to_all(payload, "lon", 0, 0, tiled=True)
    temporal, first, last = pl.pallas_call(
        mix_kernel,
        in_specs=[hbm] * 3,
        out_specs=[vmem] * 3,
        out_shape=[struct((ROWS, 512), BF16), struct((8, 512), BF16), struct((8, 512), BF16)],
        scratch_shapes=[
            pltpu.VMEM((N_LON, 8, 128), BF16),
            pltpu.VMEM((2, CHUNK, 128), BF16),
            pltpu.VMEM((ROWS, 256), F32),
            pltpu.VMEM((3, LAT, LAT), BF16),
            pltpu.VMEM((N_LON * 8, 128), F32),
            pltpu.SemaphoreType.DMA((5,)),
        ],
        compiler_params=pltpu.CompilerParams(vmem_limit_bytes=56 * 1024 * 1024),
        name="mix",
    )(arrived, own, temporal_taps_weight)
    ring = [(b, (b + 1) % N_BAND) for b in range(N_BAND)]
    above = lax.ppermute(last, "band", ring)
    below = lax.ppermute(first, "band", [(b, a) for a, b in ring])
    decoded = pl.pallas_call(
        block_kernel,
        in_specs=[anywhere] * 3 + [hbm] * 6,
        out_specs=hbm,
        out_shape=struct((2 * COLS, 2 * ROWS, CH), BF16),
        scratch_shapes=[
            pltpu.VMEM((ROWS, 512), BF16),
            pltpu.VMEM((2, 8, 512), BF16),
            pltpu.VMEM((2, CH), F32),
            pltpu.VMEM((2, CH), F32),
            pltpu.VMEM((3, 128, CH), BF16),
            pltpu.VMEM((2, 3, 3 * CH, CH), BF16),
            pltpu.VMEM((9, CH, CH), BF16),
            pltpu.VMEM((2, 2, 4 * CH, CH), BF16),
            pltpu.VMEM((2, 4, 3, CH, CH), BF16),
            pltpu.VMEM((2, 3, CH, CH), BF16),
            pltpu.VMEM((48 * LOW, 128), F32),
            pltpu.VMEM((40 * LOW, CH), F32),
            pltpu.VMEM((40 * LOW, 3 * CH), BF16),
            pltpu.VMEM((38 * LOW, 3 * CH), BF16),
            pltpu.VMEM((36 * HIGH, 2 * CH), BF16),
            pltpu.VMEM((2, 44 * LOW, 128), F32),
            pltpu.VMEM((68 * HIGH, 4 * CH), BF16),
            pltpu.VMEM((68 * HIGH, 2 * CH), BF16),
            pltpu.VMEM((66 * HIGH, 4 * CH), BF16),
            pltpu.VMEM((2, 2, 24 * HIGH, 128), F32),
            pltpu.VMEM((2 * COLS, 2 * ROWS, CH), BF16),
            pltpu.SemaphoreType.DMA((17,)),
            pltpu.SemaphoreType.DMA((4,)),
        ],
        compiler_params=pltpu.CompilerParams(vmem_limit_bytes=56 * 1024 * 1024),
        name="block",
    )(
        temporal,
        above,
        below,
        latent_norm_gains,
        upper_norm_gains,
        input_weight.reshape(3, 48, CH),
        latent_conv_weights.reshape(2, 3, 3 * CH, CH),
        upsampled_weight,
        upper_conv_weights.reshape(2, 3, 3, CH, CH),
    )
    return decoded.transpose(1, 0, 2)


def solution(mesh):
    in_specs = (
        P("band", "lon", None),
        P("band", None),
        P(None, "band", "lon"),
        P(),
        P(),
        P(),
        P(),
        P(),
        P(),
        P(),
        P(),
    )
    out_specs = P("band", "lon", None)
    return jax.shard_map(shards, mesh=mesh, in_specs=in_specs, out_specs=out_specs, check_vma=False)
```

```python
import functools

import jax
import jax.numpy as jnp
from jax import lax
from jax.experimental import pallas as pl
from jax.experimental.pallas import tpu as pltpu
from jax.sharding import PartitionSpec as P

F32 = jnp.float32
BF16 = jnp.bfloat16

N_LON = 32
N_BAND = 4
ROWS = 32
COLS = 15
LAT = 16
CH = 256
HALO = 5
TOKEN = 480 * LAT
LANES = COLS * LAT
EDGE = HALO * LAT
WINDOW = LANES + 2 * EDGE
CHUNK = 24


def window_start(lon):
    return (LANES * lon - EDGE) // 128


def window_offset(lon):
    return (LANES * lon - EDGE) % 128


def iota(shape, dim):
    return lax.broadcasted_iota(jnp.int32, shape, dim)


def block_diagonal(tap):
    wide = jnp.concatenate([tap.astype(F32)] * (128 // LAT), axis=1)
    full = jnp.concatenate([wide] * (128 // LAT), axis=0)
    same = iota((128, 128), 0) // LAT == iota((128, 128), 1) // LAT
    return jnp.where(same, full, 0.0).astype(BF16)


def pack_kernel(index_ref, slot_ref, token_ref, cache_ref, taps_ref, send_ref, own_ref, x_ref):
    lon = lax.axis_index("lon")
    row = jnp.int32(0)
    for r in range(ROWS):
        row = jnp.where(index_ref[0, r] == lon, r, row)
    tag = row.astype(F32)
    for k in range(TOKEN // 128):
        piece = token_ref[0, :, 128 * k : 128 * k + 128].astype(F32)
        x_ref[k : k + 1, :] = piece
        if k < 4:
            x_ref[60 + k : 61 + k, :] = piece
    place = iota((8, 128), 0) * 128 + iota((8, 128), 1)
    for target in range(N_LON):
        start = window_start(target) % 60
        spot = (window_offset(target) + WINDOW) % 512
        tile = x_ref[start : start + 8, :]
        send_ref[target, 0:8, :] = jnp.where(place == spot, tag, tile).astype(BF16)

    diagonals = [block_diagonal(taps_ref[t]) for t in (1, 2)]
    mixed = jnp.zeros((2 * ROWS, 128), F32)
    for t in range(2):
        frame = cache_ref[slot_ref[t]]
        frame = jnp.concatenate([frame, jnp.zeros((ROWS, 256 - LANES), BF16)], axis=1)
        stacked = jnp.concatenate([frame[:, :128], frame[:, 128:]], axis=0)
        mixed = mixed + jnp.dot(stacked, diagonals[t], preferred_element_type=F32)
    own = jnp.concatenate([mixed[:ROWS], mixed[ROWS:]], axis=1)
    own_ref[...] = own

    for d_lon, v in ((-1, own[:, :EDGE]), (1, own[:, LANES - EDGE : LANES])):
        top = jnp.concatenate([v[:16, :], v[16:, : 128 - EDGE]], axis=1)
        low = jnp.concatenate(
            [v[16 + 4 * m : 20 + 4 * m, 128 - EDGE : EDGE] for m in range(4)], axis=1
        )
        full = jnp.concatenate([jnp.zeros((4, 128), F32), top, low], axis=0)
        to = lax.rem(lon + d_lon + N_LON, N_LON)
        first = send_ref[to, 0:8, :].astype(F32)
        send_ref[to, 0:8, :] = jnp.where(iota((8, 128), 0) < 4, first, full[:8]).astype(BF16)
        send_ref[to, 8:CHUNK, :] = full[8:].astype(BF16)


def mix_kernel(
    got_hbm,
    own_hbm,
    taps_hbm,
    out_ref,
    first_ref,
    last_ref,
    got_ref,
    near_ref,
    own_ref,
    taps_ref,
    tok_ref,
    sem,
):
    lon = lax.axis_index("lon")
    copies = [
        pltpu.make_async_copy(got_hbm.at[:, 0:8], got_ref, sem.at[0]),
        pltpu.make_async_copy(taps_hbm, taps_ref, sem.at[1]),
        pltpu.make_async_copy(own_hbm, own_ref, sem.at[2]),
    ]
    for n in range(2):
        source = lax.rem(lon + 2 * n - 1 + N_LON, N_LON)
        copies.append(pltpu.make_async_copy(got_hbm.at[source], near_ref.at[n], sem.at[3 + n]))
    for copy in copies:
        copy.start()
    for copy in copies:
        copy.wait()

    tok_ref[...] = got_ref[...].astype(F32).reshape(N_LON * 8, 128)
    x = jnp.concatenate([tok_ref[pl.ds(k, N_LON, stride=8), :] for k in range(4)], axis=1)
    offset = lax.rem(LANES * lon + (128 - EDGE), 128)
    x = pltpu.roll(x, lax.rem(512 - offset, 512), axis=1)
    tag = x[:, WINDOW : WINDOW + 1].astype(jnp.int32)
    select = jnp.where(tag == iota((N_LON, 128), 1), 1.0, 0.0)
    select = jnp.concatenate([select, jnp.zeros((128 - N_LON, 128), F32)], axis=0)
    select = select.T[:ROWS, :N_LON].astype(BF16)
    latent = jnp.dot(select, x.astype(BF16), preferred_element_type=F32).astype(BF16)

    def side(n):
        c = near_ref[n].astype(F32)[4:]
        low = jnp.concatenate([c[16:20, 32 * k : 32 * k + 32] for k in range(4)], axis=0)
        low = jnp.concatenate([c[:16, EDGE:], low], axis=1)
        return jnp.concatenate([c[:16, :EDGE], low], axis=0)

    cached = jnp.concatenate(
        [side(0), own_ref[:, :LANES], side(1), jnp.zeros((ROWS, 512 - WINDOW), F32)], axis=1
    )
    stacked = jnp.concatenate([latent[:, 128 * k : 128 * k + 128] for k in range(4)], axis=0)
    fresh = jnp.dot(stacked, block_diagonal(taps_ref[0]), preferred_element_type=F32)
    fresh = jnp.concatenate([fresh[ROWS * k : ROWS * k + ROWS] for k in range(4)], axis=1)
    temporal = jnp.where(iota((ROWS, 512), 1) < WINDOW, fresh + cached, 0.0)
    out_ref[...] = temporal.astype(BF16)
    first_ref[...] = temporal[:8].astype(BF16)
    last_ref[...] = temporal[ROWS - 8 :].astype(BF16)


def activate(values, gain):
    mean = jnp.sum(values * values, axis=-1, keepdims=True) * (1.0 / CH)
    half = values * lax.rsqrt(mean + 1e-06) * (0.5 * gain)
    return half * jnp.tanh(half) + half


def roll_rows(values, by):
    return pltpu.roll(values, by % values.shape[0], axis=0)


def cuts(rows, pieces):
    ends = [rows * k // pieces for k in range(pieces + 1)]
    return [(low, high - low) for low, high in zip(ends[:-1], ends[1:])]


LOW = 24
HIGH = 16


def block_kernel(
    temporal_hbm,
    above_hbm,
    below_hbm,
    low_gain_hbm,
    high_gain_hbm,
    w_in_hbm,
    w_low_hbm,
    w_up_hbm,
    w_high_hbm,
    out_hbm,
    temporal_ref,
    rim_ref,
    low_gain_ref,
    high_gain_ref,
    w_in,
    w_low,
    w_up,
    w_phase,
    w_high,
    w_mid,
    u_ref,
    open_ref,
    a1_ref,
    a2_ref,
    low_ref,
    lowf_ref,
    s1_ref,
    raw_ref,
    s2_ref,
    mix_ref,
    out_ref,
    in_sem,
    out_sem,
):
    band = lax.axis_index("band")
    copies = [pltpu.make_async_copy(w_in_hbm.at[p], w_in.at[p, 0:48], in_sem.at[p]) for p in range(3)]
    copies.append(pltpu.make_async_copy(w_low_hbm.at[0], w_low.at[0], in_sem.at[3]))
    copies.append(pltpu.make_async_copy(w_low_hbm.at[1], w_low.at[1], in_sem.at[4]))
    copies.append(pltpu.make_async_copy(w_up_hbm, w_up, in_sem.at[5]))
    for n in range(2):
        for k in range(3):
            target = w_mid.at[n] if k == 1 else w_high.at[n, k // 2 * 3]
            pair = (w_high_hbm.at[n, :, k], target)
            copies.append(pltpu.make_async_copy(*pair, in_sem.at[6 + 3 * n + k]))
    small = [
        pltpu.make_async_copy(source, target, in_sem.at[12 + n])
        for n, (source, target) in enumerate(
            (
                (temporal_hbm, temporal_ref),
                (above_hbm, rim_ref.at[0]),
                (below_hbm, rim_ref.at[1]),
                (low_gain_hbm, low_gain_ref),
                (high_gain_hbm, high_gain_ref),
            )
        )
    ]
    for copy in small + copies:
        copy.start()
    w_in[:, 48:128, :] = jnp.zeros((3, 80, CH), BF16)

    for copy in small:
        copy.wait()
    above = jnp.where(band > 0, rim_ref[0].astype(F32), 0.0)
    below = jnp.where(band < N_BAND - 1, rim_ref[1].astype(F32), 0.0)
    temporal = jnp.concatenate(
        [
            above[8 - HALO :],
            temporal_ref[...].astype(F32),
            below[:HALO],
            jnp.zeros((6, 512), F32),
        ],
        axis=0,
    )

    wide = jnp.concatenate([temporal, jnp.zeros((48, 128), F32)], axis=1)
    for j in range(LOW):
        piece = wide[:, 128 * (j // 8) : 128 * (j // 8) + 256]
        turn = LAT * (j % 8)
        if turn:
            piece = pltpu.roll(piece, 256 - turn, axis=1)
        u_ref[pl.ds(j, 48, stride=LOW), :] = piece[:, :128]

    def outside(value, pitch, row, top, bottom, rows):
        count = value.shape[0] // pitch
        above = min(max(top - row, 0), count)
        below = min(max(row + count - (rows - bottom), 0), count)
        parts = []
        if above:
            parts.append(jnp.where(band == 0, 0.0, value[: above * pitch]))
        parts.append(value[above * pitch : (count - below) * pitch])
        if below:
            parts.append(jnp.where(band == N_BAND - 1, 0.0, value[(count - below) * pitch :]))
        return parts[0] if len(parts) == 1 else jnp.concatenate(parts, axis=0)

    def conv(ref, pitch, row, count, lane, weight):
        total = None
        for p in range(3):
            part = jnp.dot(
                ref[(row + p) * pitch : (row + p + count) * pitch, lane : lane + 3 * CH],
                weight[p],
                preferred_element_type=F32,
            )
            total = part if total is None else total + part
        return total

    def spread(act, ref, row):
        rows = slice(row * LOW, row * LOW + act.shape[0])
        ref[rows, 0:CH] = roll_rows(act, 1).astype(BF16)
        ref[rows, CH : 2 * CH] = act.astype(BF16)
        ref[rows, 2 * CH :] = roll_rows(act, -1).astype(BF16)

    tasks = []

    def task(product, finish, wait=None):
        tasks.append((product, finish, wait))

    for row, count in cuts(40, 3):

        def product(row=row, count=count):
            lhs = [u_ref[(row + p) * LOW : (row + p + count) * LOW, :] for p in range(3)]
            lhs = jnp.concatenate(lhs, axis=1).astype(BF16)
            return jnp.dot(lhs, w_in[...].reshape(384, CH), preferred_element_type=F32)

        def finish(value, row=row, count=count):
            value = value.astype(BF16).astype(F32)
            open_ref[row * LOW : (row + count) * LOW, :] = value
            act = activate(value, low_gain_ref[0:1, :])
            spread(outside(act, LOW, row, 4, 4, 40), a1_ref, row)

        task(product, finish, copies[:3] if row == 0 else None)

    for row, count in cuts(38, 3):

        def product(row=row, count=count):
            return conv(a1_ref, LOW, row, count, 0, w_low.at[0])

        def finish(value, row=row):
            act = activate(value, low_gain_ref[1:2, :])
            spread(outside(act, LOW, row, 3, 3, 38), a2_ref, row)

        task(product, finish, copies[3:4] if row == 0 else None)

    for row, count in cuts(36, 3):

        def product(row=row, count=count):
            return conv(a2_ref, LOW, row, count, 0, w_low.at[1])

        def finish(value, row=row, count=count):
            low = open_ref[(row + 2) * LOW : (row + 2 + count) * LOW, :] + value
            low = outside(low.astype(BF16).astype(F32), LOW, row, 2, 2, 36)
            for half in range(2):
                lowf_ref[half, row * LOW : (row + count) * LOW, :] = low[
                    :, 128 * half : 128 * half + 128
                ]
            for k in range(2):
                part = roll_rows(low, -(3 + k)).reshape(count, LOW, CH)[:, :HIGH]
                low_ref[row * HIGH : (row + count) * HIGH, CH * k : CH * k + CH] = part.reshape(
                    count * HIGH, CH
                ).astype(BF16)

        task(product, finish, copies[4:5] if row == 0 else None)

    def phase_weights(a, odd):
        for r in range(2):
            taps = ((0,), (1, 2)) if a == 0 else ((0, 1), (2,))
            sides = ((0, 1), (2,)) if odd else ((0,), (1, 2))
            for c in range(2):
                total = None
                for p in taps[r]:
                    for q in sides[c]:
                        one = w_up[3 * p + q].astype(F32)
                        total = one if total is None else total + one
                at = (2 * r + c) * CH
                w_phase[a, odd, at : at + CH, :] = total.astype(BF16)

    def sum_weights(n, p):
        outer = w_high[n, 0, p].astype(F32) + w_high[n, 3, p].astype(F32)
        inner = w_mid[n, p].astype(F32)
        w_high[n, 1, p] = (0.5 * (outer + inner)).astype(BF16)
        w_high[n, 2, p] = (0.5 * (outer - inner)).astype(BF16)

    beside = {}
    for k in range(4):
        beside[3 + k] = (copies[5:6] if k == 0 else (), phase_weights, (k // 2, k % 2))
    for p in range(3):
        beside[7 + p] = (copies[6:9] if p == 0 else (), sum_weights, (0, p))
        beside[17 + p] = (copies[9:12] if p == 0 else (), sum_weights, (1, p))

    held = []

    def quads(evens, odd, odd_next):
        even_last, even = evens
        parts = (even_last - even, odd + even, even - odd, odd - odd_next)
        return [part.astype(BF16) for part in parts]

    def pairs(ref, row, count, weight):
        m = []
        for k in range(4):
            total = None
            for p in range(3):
                part = jnp.dot(
                    ref[(row + p) * HIGH : (row + p + count) * HIGH, CH * k : CH * k + CH],
                    weight[k, p],
                    preferred_element_type=F32,
                )
                total = part if total is None else total + part
            m.append(total)
        return m[0] + m[1] + m[2], m[1] - m[2] - m[3]

    for n in (0, 17):
        for a in range(2):
            for odd in range(2):

                def product(n=n, a=a, odd=odd):
                    parts = []
                    for r in range(2):
                        at = n + a + r
                        col = 19 if odd else 2
                        pair = [
                            lowf_ref[half, pl.ds(at * LOW + col + c, 24, stride=LOW), :]
                            for c in range(2)
                            for half in range(2)
                        ]
                        pair = jnp.concatenate(pair, axis=1).astype(BF16)
                        main = low_ref[at * HIGH : (at + 17) * HIGH, :]
                        pad = jnp.zeros((8, 2 * CH), BF16)
                        parts.append(jnp.concatenate([main, pair, pad], axis=0))
                    return jnp.dot(
                        jnp.concatenate(parts, axis=1),
                        w_phase[a, odd],
                        preferred_element_type=F32,
                    )

                def finish(value, n=n, a=a, odd=odd):
                    value = value[: 17 * HIGH + 24].astype(BF16)
                    act = activate(value.astype(F32), high_gain_ref[0:1, :])
                    border = act[17 * HIGH :]
                    act = act[: 17 * HIGH]
                    turned = roll_rows(act, -1 if odd else 1)
                    for half in range(2):
                        lanes = slice(128 * half, 128 * half + 128)
                        mix_ref[odd, half, 0 : 17 * HIGH, :] = turned[:, lanes]
                        mix_ref[odd, half, pl.ds(15 if odd else 0, 24, stride=HIGH), :] = border[
                            :, lanes
                        ]
                    turned = jnp.concatenate(
                        [mix_ref[odd, half, 0 : 17 * HIGH, :] for half in range(2)], axis=1
                    )
                    act = outside(act, HIGH, n, 1, 1, 34)
                    turned = outside(turned, HIGH, n, 1, 1, 34)
                    if odd:
                        parts = quads(held.pop(), act, turned)
                    else:
                        held.append((turned, act))
                    for i in range(17):
                        rows = slice(i * HIGH, (i + 1) * HIGH)
                        at = (2 * (n + i) + a) * HIGH
                        if odd:
                            for k in range(4):
                                s1_ref[at : at + HIGH, CH * k : CH * k + CH] = parts[k][rows]
                        raw_ref[at : at + HIGH, CH * odd : CH * odd + CH] = value[rows]

                task(product, finish)

    for row, count in cuts(66, 6):

        def product(row=row, count=count):
            return pairs(s1_ref, row, count, w_high.at[0])

        def finish(values, row=row, count=count):
            odd, even = (
                outside(activate(value, high_gain_ref[1:2, :]), HIGH, row, 1, 1, 66)
                for value in values
            )
            parts = quads((roll_rows(even, 1), even), odd, roll_rows(odd, -1))
            for k in range(4):
                s2_ref[row * HIGH : (row + count) * HIGH, CH * k : CH * k + CH] = parts[k]

        task(product, finish)

    outs = []
    for n, row in enumerate(range(0, 64, 16)):

        def product(row=row):
            return pairs(s2_ref, row, 16, w_high.at[1])

        def finish(values, n=n, row=row):
            rows = slice((row + 2) * HIGH, (row + 18) * HIGH)
            for odd in range(2):
                value = values[1 - odd] + raw_ref[rows, odd * CH : odd * CH + CH].astype(F32)
                value = jnp.swapaxes(value.reshape(16, HIGH, CH), 0, 1).astype(BF16)
                for j in range(COLS):
                    out_ref[2 * j + odd, row : row + 16, :] = value[j + odd]
            copy = pltpu.make_async_copy(
                out_ref.at[:, row : row + 16], out_hbm.at[:, row : row + 16], out_sem.at[n]
            )
            copy.start()
            outs.append(copy)

        task(product, finish)

    before = None
    for number, (product, finish, wait) in enumerate(tasks):
        for copy in wait or ():
            copy.wait()
        value = product()
        if before is not None:
            before[0](before[1])
        before = (finish, value)
        if number in beside:
            arrive, work, which = beside[number]
            for copy in arrive:
                copy.wait()
            work(*which)
    before[0](before[1])
    for copy in outs:
        copy.wait()


def shards(
    denoised_tokens,
    sequence_row_index,
    latent_frame_cache,
    cache_slot_order,
    temporal_taps_weight,
    input_weight,
    latent_conv_weights,
    upsampled_weight,
    upper_conv_weights,
    latent_norm_gains,
    upper_norm_gains,
):
    struct = jax.ShapeDtypeStruct
    vmem = pl.BlockSpec(memory_space=pltpu.VMEM)
    smem = pl.BlockSpec(memory_space=pltpu.SMEM)
    hbm = pl.BlockSpec(memory_space=pltpu.HBM)
    anywhere = pl.BlockSpec(memory_space=pl.ANY)
    payload, own = pl.pallas_call(
        pack_kernel,
        in_specs=[smem, smem, vmem, vmem, vmem],
        out_specs=[vmem, vmem],
        out_shape=[struct((N_LON, CHUNK, 128), BF16), struct((ROWS, 256), F32)],
        scratch_shapes=[pltpu.VMEM((72, 128), F32)],
        name="pack",
    )(
        sequence_row_index,
        cache_slot_order,
        denoised_tokens,
        latent_frame_cache,
        temporal_taps_weight,
    )
    arrived = lax.all_to_all(payload, "lon", 0, 0, tiled=True)
    temporal, first, last = pl.pallas_call(
        mix_kernel,
        in_specs=[hbm] * 3,
        out_specs=[vmem] * 3,
        out_shape=[struct((ROWS, 512), BF16), struct((8, 512), BF16), struct((8, 512), BF16)],
        scratch_shapes=[
            pltpu.VMEM((N_LON, 8, 128), BF16),
            pltpu.VMEM((2, CHUNK, 128), BF16),
            pltpu.VMEM((ROWS, 256), F32),
            pltpu.VMEM((3, LAT, LAT), BF16),
            pltpu.VMEM((N_LON * 8, 128), F32),
            pltpu.SemaphoreType.DMA((5,)),
        ],
        compiler_params=pltpu.CompilerParams(vmem_limit_bytes=56 * 1024 * 1024),
        name="mix",
    )(arrived, own, temporal_taps_weight)
    ring = [(b, (b + 1) % N_BAND) for b in range(N_BAND)]
    above = lax.ppermute(last, "band", ring)
    below = lax.ppermute(first, "band", [(b, a) for a, b in ring])
    decoded = pl.pallas_call(
        block_kernel,
        in_specs=[anywhere] * 3 + [hbm] * 6,
        out_specs=hbm,
        out_shape=struct((2 * COLS, 2 * ROWS, CH), BF16),
        scratch_shapes=[
            pltpu.VMEM((ROWS, 512), BF16),
            pltpu.VMEM((2, 8, 512), BF16),
            pltpu.VMEM((2, CH), F32),
            pltpu.VMEM((2, CH), F32),
            pltpu.VMEM((3, 128, CH), BF16),
            pltpu.VMEM((2, 3, 3 * CH, CH), BF16),
            pltpu.VMEM((9, CH, CH), BF16),
            pltpu.VMEM((2, 2, 4 * CH, CH), BF16),
            pltpu.VMEM((2, 4, 3, CH, CH), BF16),
            pltpu.VMEM((2, 3, CH, CH), BF16),
            pltpu.VMEM((48 * LOW, 128), F32),
            pltpu.VMEM((40 * LOW, CH), F32),
            pltpu.VMEM((40 * LOW, 3 * CH), BF16),
            pltpu.VMEM((38 * LOW, 3 * CH), BF16),
            pltpu.VMEM((36 * HIGH, 2 * CH), BF16),
            pltpu.VMEM((2, 44 * LOW, 128), F32),
            pltpu.VMEM((68 * HIGH, 4 * CH), BF16),
            pltpu.VMEM((68 * HIGH, 2 * CH), BF16),
            pltpu.VMEM((66 * HIGH, 4 * CH), BF16),
            pltpu.VMEM((2, 2, 24 * HIGH, 128), F32),
            pltpu.VMEM((2 * COLS, 2 * ROWS, CH), BF16),
            pltpu.SemaphoreType.DMA((17,)),
            pltpu.SemaphoreType.DMA((4,)),
        ],
        compiler_params=pltpu.CompilerParams(vmem_limit_bytes=56 * 1024 * 1024),
        name="block",
    )(
        temporal,
        above,
        below,
        latent_norm_gains,
        upper_norm_gains,
        input_weight.reshape(3, 48, CH),
        latent_conv_weights.reshape(2, 3, 3 * CH, CH),
        upsampled_weight,
        upper_conv_weights.reshape(2, 3, 3, CH, CH),
    )
    return decoded.transpose(1, 0, 2)


def solution(mesh):
    in_specs = (
        P("band", "lon", None),
        P("band", None),
        P(None, "band", "lon"),
        P(),
        P(),
        P(),
        P(),
        P(),
        P(),
        P(),
        P(),
    )
    out_specs = P("band", "lon", None)
    return jax.shard_map(shards, mesh=mesh, in_specs=in_specs, out_specs=out_specs, check_vma=False)
```
